256 devices in a mesh: gx: 32 (over z, x), yz: 8 (over y, core).
Axes of the slice: x: 4, y: 4, z: 8, core: 2. Of those that a mesh axis runs over, the one named last changes fastest.
Arguments:
- tensor_slabs: bfloat16 [2048, 32, 1024], P('gx', 'yz'), may hold values from -6 to 6
- slab_counts: int32 [8], replicated, may hold values from 1 to 4, 16 in all
- column_scale: float32 [16, 1024], replicated, may hold values from -6 to 6
- samples: int32 [16, 256], replicated, may hold values from 0 to 1023
Outputs:
- basis_factor: float32 [2048, 256], P('gx')
- core_tensor: bfloat16 [256, 32, 1024], P(None, 'yz', 'gx')
The draws below stay inside these ranges and needn't reach their ends.
Inputs may be any that keep to these rules, and one draw needn't show every extreme that they name: `slab_counts`: the counts sum to 16; the largest is exactly 4. Slots at or beyond an index's count hold no slab and are not read.
All inputs are finite; a program needn't handle non-finite values.
Results may differ from the reference program's by a relative error of at most 0.0057.
Values may be sent and summed in bfloat16 or wider, within the bound.
No kernel may reach another device: no remote copies, remote signals or barrier semaphores. Data moves between devices by JAX's collectives and lax.ppermute only.
A program may use at most 64 MiB of HBM per device.

```python
import math
import jax
import jax.numpy as jnp
import numpy as np
from jax import lax

B = 1024
SKETCH = 256
SLOT_DEV = 4
NY = 16
SLOTS = 32
ROWS = 2048
N_YZ = 8


def touch_ends(array, stream_key, least, top_value):
    longest = array.shape.index(max(array.shape))
    spots = []
    for shift in (0, 1):
        where = [jax.random.randint(jax.random.fold_in(stream_key, axis), (), 0, length) for axis, length in enumerate(array.shape)]
        where[longest] = (where[longest] + shift) % array.shape[longest]
        spots.append(tuple(where))
    return array.at[spots[0]].set(least).at[spots[1]].set(top_value)


def level_of(stream_key, shape, cuts, low, high):
    level = 1.0
    for dim, blocks in cuts:
        steps = jax.random.uniform(jax.random.fold_in(jax.random.fold_in(stream_key, 6), dim), (blocks,), jnp.float32, low / len(cuts), high / len(cuts))
        level = level * jnp.repeat(jnp.exp(steps), shape[dim] // blocks).reshape((-1,) + (1,) * (len(shape) - 1 - dim))
    return level


def split_up(number_of, total, bound, slope):
    loads = [(1 << 20) // math.isqrt(standing ** slope) + 1 for standing in range(2, number_of + 1)]
    rest, given = total - bound - (number_of - 1), [1] * (number_of - 1)
    while rest > 0:
        candidates = [i for i in range(number_of - 1) if given[i] < bound]
        mass, left = sum([loads[i] for i in candidates]), rest
        for i in candidates:
            extra = min(bound - given[i], max(1, left * loads[i] // mass), rest)
            given[i] = given[i] + extra
            rest = rest - extra
    return np.array([bound] + given)


def ragged(stream_key, count, total, most, lean):
    if count == 2:
        one = jax.random.randint(stream_key, (), max(1, total - most), min(most, total - 1) + 1)
        return jnp.stack([one, total - one])
    tallies = jnp.asarray(split_up(count, total, most, lean), jnp.int32)
    pairs = (count - 1) // 2
    source_of, sink = tallies[1:1 + 2 * pairs:2], tallies[2:2 + 2 * pairs:2]
    room = jnp.minimum(source_of - 1, most - sink)
    shifted = jax.random.randint(jax.random.fold_in(stream_key, 1), (pairs,), 0, 1 << 20) % (room + 1)
    tallies = tallies.at[1:1 + 2 * pairs:2].set(source_of - shifted).at[2:2 + 2 * pairs:2].set(sink + shifted)
    return tallies[jax.random.permutation(jax.random.fold_in(stream_key, 2), count)]


def centred(own_key, shape, spread, limit, cuts=(), kind=jnp.bfloat16):
    array = jax.random.normal(own_key, shape, jnp.float32) * spread
    if len(cuts) > 0:
        array = level_of(own_key, shape, cuts, -0.22, 0.18) * array
    return jnp.clip(array, min=-limit, max=limit).astype(kind)


def setup_inputs(seed: int = 0) -> dict:
    splits = jax.random.split(jax.random.key(seed), 5)
    tensor_slabs = centred(splits[0], (ROWS, SLOTS, B), 1.0, 6.0, ((0, 32), (1, 8)))
    slab_counts = ragged(splits[1], N_YZ, NY, SLOT_DEV, 2).astype(jnp.int32)
    column_scale = centred(splits[2], (NY, B), 1.0, 6.0, (), jnp.float32)
    samples = touch_ends(jax.random.randint(splits[3], (NY, SKETCH), 0, B), jax.random.fold_in(splits[3], 1), 0, B - 1).astype(jnp.int32)
    return {"tensor_slabs": tensor_slabs, "slab_counts": slab_counts, "column_scale": column_scale, "samples": samples}


def hadamard_columns(picked, length):
    index_rows = jnp.arange(length, dtype=jnp.int32)[:, None]
    picked_row = picked.astype(jnp.int32)[None, :]
    parity = jnp.zeros((length, picked.shape[0]), jnp.int32)
    for bit_place in range(length.bit_length() - 1):
        parity = parity + jnp.bitwise_and(jnp.right_shift(index_rows, bit_place), 1) * jnp.bitwise_and(jnp.right_shift(picked_row, bit_place), 1)
    return (1 - 2 * (parity % 2)).astype(jnp.bfloat16)

def reference(tensor_slabs, slab_counts, column_scale, samples):
    counts = slab_counts.astype(jnp.int32)
    offsets = jnp.cumsum(counts).astype(jnp.int32) - counts
    pad_scale = jnp.concatenate([column_scale, jnp.zeros((SLOT_DEV, B), column_scale.dtype)], 0)
    pad_samples = jnp.concatenate([samples.astype(jnp.int32), jnp.zeros((SLOT_DEV, SKETCH), jnp.int32)], 0)

    def add_slab(total, slot_number):
        device_number = slot_number // SLOT_DEV
        position = slot_number % SLOT_DEV
        slab_index = offsets[device_number] + position
        alive = (position < counts[device_number]).astype(total.dtype)
        piece = lax.dynamic_index_in_dim(tensor_slabs, slot_number, 1, keepdims=False)
        scaled = (piece.astype(pad_scale.dtype) * pad_scale[slab_index][None, :]).astype(jnp.bfloat16)
        hadamard_part = hadamard_columns(pad_samples[slab_index], B)
        return (total + alive * jnp.dot(scaled.astype(jnp.float32), hadamard_part.astype(jnp.float32), preferred_element_type=jnp.float32).astype(total.dtype), None)
    start = jnp.zeros((ROWS, SKETCH), jnp.float32)
    summed = lax.scan(add_slab, start, jnp.arange(SLOTS, dtype=jnp.int32))[0]
    sketch = summed * (1.0 / math.sqrt(NY * B))
    gram_matrix = jnp.dot(sketch.T, sketch, precision=lax.Precision.HIGHEST)
    cholesky_factor = jnp.linalg.cholesky(gram_matrix)
    basis_factor = lax.linalg.triangular_solve(cholesky_factor, sketch, left_side=False, lower=True, transpose_a=True)
    factor_bf = basis_factor.astype(jnp.bfloat16)
    flattened = tensor_slabs.reshape(ROWS, SLOTS * B)
    projected = jnp.dot(factor_bf.T.astype(jnp.float32), flattened.astype(jnp.float32), preferred_element_type=jnp.float32).reshape(SKETCH, SLOTS, B)
    slot_numbers = jnp.arange(SLOTS, dtype=jnp.int32)
    slot_alive = (slot_numbers % SLOT_DEV < counts[slot_numbers // SLOT_DEV]).astype(projected.dtype)
    core_tensor = (projected * slot_alive[None, :, None]).astype(jnp.bfloat16)
    return (basis_factor, core_tensor)
```

```python
import functools

import jax
import jax.numpy as jnp
from jax import lax
from jax.experimental import pallas as pl
from jax.experimental.pallas import tpu as pltpu
from jax.sharding import PartitionSpec as P

F32, BF16, I32 = jnp.float32, jnp.bfloat16, jnp.int32
NN, NT, TN = ((1,), (0,)), ((1,), (1,)), ((0,), (0,))
HIGHEST = lax.Precision.HIGHEST
AHEAD = 10
BLOCK = 64


def dot(a, b, dims, precision=None):
    return lax.dot_general(
        a, b, (dims, ((), ())), precision=precision, preferred_element_type=F32
    )


def signs(rows, picked):
    both = lax.broadcasted_iota(I32, (rows, picked.shape[1]), 0) & picked
    both = both ^ (both >> 4)
    both = both ^ (both >> 2)
    both = both ^ (both >> 1)
    return (1 - 2 * (both & 1)).astype(F32)


def own_slabs(counts_ref, index, groups):
    offset = jnp.int32(0)
    for group in range(groups):
        offset = offset + jnp.where(group < index, counts_ref[group], 0)
    return offset, counts_ref[index]


def sketch_kernel(tensor_ref, counts_ref, scale_ref, samples_ref, keep_ref, send_ref, moved_ref,
                  hadamard_ref, total_ref):
    rows, slots, width = tensor_ref.shape
    total_slabs, sketch = samples_ref.shape
    index = lax.axis_index("yz")
    offset, count = own_slabs(counts_ref, index, counts_ref.shape[0])
    lines = tensor_ref[...].astype(F32).reshape(rows * slots, width).astype(BF16)
    at = lax.broadcasted_iota(I32, (rows * slots, rows * slots), 0)
    of = lax.broadcasted_iota(I32, (rows * slots, rows * slots), 1)
    pick = ((at % rows) * slots + at // rows == of).astype(F32).astype(BF16)
    by_slot = dot(pick, lines, NN)
    total = jnp.zeros((rows, sketch), F32)
    for slot in range(slots):
        slab = jnp.minimum(offset + slot, total_slabs - 1)
        picked = samples_ref[pl.ds(slab, 1), :]
        low = signs(32, picked & 31)
        high = signs(width // 32, picked >> 5)
        for part in range(width // 32):
            hadamard_ref[slot, pl.ds(part * 32, 32), :] = (low * high[part : part + 1, :]).astype(BF16)
        piece = by_slot[slot * rows : (slot + 1) * rows]
        scaled = (piece * scale_ref[pl.ds(slab, 1), :]).astype(BF16)
        term = dot(scaled, hadamard_ref[slot], NN)
        total = total + jnp.where(slot < count, term, 0.0)
    total_ref[...] = total * (1.0 / (total_slabs * width) ** 0.5)
    core = index % 2
    half = rows // 2
    keep_ref[...] = total_ref[pl.ds(pl.multiple_of(core * half, half), half), :]
    send_ref[...] = total_ref[pl.ds(pl.multiple_of((1 - core) * half, half), half), :]
    chunk = 128 // slots
    for chunk_index in range(width // chunk):
        start = chunk_index * chunk
        moved_ref[chunk_index] = jnp.concatenate(
            [by_slot[s * rows : (s + 1) * rows, start : start + chunk] for s in range(slots)], axis=1
        ).astype(BF16)


def sketch_parts(tensor, counts, scale, samples):
    rows, slots, width = tensor.shape
    sketch = samples.shape[1]
    chunks = width * slots // 128
    vmem = pl.BlockSpec(memory_space=pltpu.VMEM)
    half = jax.ShapeDtypeStruct((rows // 2, sketch), F32)
    return pl.pallas_call(
        sketch_kernel,
        out_shape=(half, half, jax.ShapeDtypeStruct((chunks, rows, 128), BF16)),
        in_specs=[vmem, pl.BlockSpec(memory_space=pltpu.SMEM), vmem, vmem],
        out_specs=(vmem, vmem, vmem),
        scratch_shapes=[pltpu.VMEM((slots, width, sketch), BF16), pltpu.VMEM((rows, sketch), F32)],
        name="sketch",
    )(tensor, counts, scale, samples)


def block_inverse(tiles):
    count = len(tiles)
    size = 8 * count
    lines = list(tiles)
    sub = lax.broadcasted_iota(I32, (8, 128), 0)
    lane = lax.broadcasted_iota(I32, (8, 128), 1)

    def row_of(tile, at):
        return jnp.broadcast_to(tile[at : at + 1, :], (8, 128))

    def column_of(tile, at):
        return jnp.broadcast_to(tile[:, at : at + 1], (8, 128))

    columns = {j: [column_of(tile, j) for tile in lines] for j in range(min(AHEAD, size))}
    pivots = [jnp.ones((8, 128), F32)] * count
    for step in range(size):
        tile, at = divmod(step, 8)
        column = columns.pop(step)
        pivot = row_of(column[tile], at)
        pivots[tile] = jnp.where(sub == at, pivot, pivots[tile])
        if step == size - 1:
            break
        inverse = 1.0 / pivot
        factors = {t: column[t] * inverse for t in range(tile, count)}
        factors[tile] = jnp.where(sub > at, factors[tile], 0.0)
        if at == 7:
            factors.pop(tile)
        for later in columns.values():
            value = row_of(later[tile], at)
            for t, factor in factors.items():
                later[t] = later[t] - factor * value
        line = jnp.where(lane == step, 1.0, row_of(lines[tile], at))
        for t, factor in factors.items():
            cleared = (lane == step) if t > tile else (lane == step) & (sub > at)
            lines[t] = jnp.where(cleared, 0.0, lines[t]) - factor * line
        new = step + AHEAD
        if new < size:
            columns[new] = [
                column_of(lines[t], new) if t >= (step + 1) // 8 else None for t in range(count)
            ]
    result = []
    for t in range(count):
        inside = jnp.where(lane == sub + 8 * t, 1.0, 0.0)
        result.append(lax.rsqrt(pivots[t]) * jnp.where(lane < sub + 8 * t, lines[t], inside))
    return jnp.concatenate(result, 0)


def factor_kernel(own_ref, other_ref, inverse_ref):
    size = own_ref.shape[1]
    inverse_ref[...] = dot(own_ref[...], own_ref[...], TN, HIGHEST) + dot(
        other_ref[...], other_ref[...], TN, HIGHEST
    )
    lanes = lax.broadcasted_iota(I32, (1, size), 1)

    def spread(block):
        return jnp.concatenate([block, jnp.zeros((BLOCK, 128 - BLOCK), F32)], 1)

    diagonal = spread(inverse_ref[0:BLOCK, 0:BLOCK])
    for start in range(0, size, BLOCK):
        end = start + BLOCK
        after = end + BLOCK
        inverse = block_inverse([diagonal[8 * t : 8 * t + 8] for t in range(BLOCK // 8)])[:, :BLOCK]
        if end < size:
            below = dot(inverse_ref[end:after, start:end], inverse, NT, HIGHEST)
            diagonal = spread(inverse_ref[end:after, end:after] - dot(below, below, NT, HIGHEST))
            rest = dot(inverse_ref[end:, start:end], inverse, NT, HIGHEST)
        inverse_ref[start:end, :] = dot(inverse, inverse_ref[start:end, :], NN, HIGHEST)
        inverse_ref[start:end, start:end] = inverse
        if end < size:
            here = (lanes >= start) & (lanes < end)
            inverse_ref[end:, :] = jnp.where(here, 0.0, inverse_ref[end:, :]) - dot(
                rest, inverse_ref[start:end, :], NN, HIGHEST
            )
    row = lax.broadcasted_iota(I32, (size, size), 0)
    column = lax.broadcasted_iota(I32, (size, size), 1)
    inverse_ref[...] = jnp.where(row >= column, inverse_ref[...], 0.0)


def inverse_factor(own, other):
    size = own.shape[1]
    vmem = pl.BlockSpec(memory_space=pltpu.VMEM)
    return pl.pallas_call(
        factor_kernel,
        out_shape=jax.ShapeDtypeStruct((size, size), F32),
        in_specs=[vmem, vmem],
        out_specs=vmem,
        name="factor",
    )(own, other)


def core_kernel(own_ref, other_ref, inverse_ref, moved_ref, counts_ref, basis_ref, core_ref, rows_ref):
    blocks, parts, line, size = rows_ref.shape
    index = lax.axis_index("yz")
    core = index % 2
    inverse = inverse_ref[...]
    for source, which in ((own_ref, core), (other_ref, 1 - core)):
        rows = dot(source[...], inverse, NT, HIGHEST).reshape(parts // 2, blocks, line, size)
        for part in range(parts // 2):
            rows_ref[:, which * (parts // 2) + part] = rows[part]
    basis_ref[...] = rows_ref[lax.axis_index("gx")].reshape(parts * line, size)
    every = rows_ref[...].reshape(blocks * parts * line, size).astype(BF16)
    moved = moved_ref[...].reshape(blocks * parts * line, 128)
    result = dot(moved, every, TN)
    slots = 4
    slot = lax.broadcasted_iota(I32, result.shape, 0) // (128 // slots)
    core_ref[...] = jnp.where(slot < counts_ref[index], result, 0.0).astype(BF16)


def core_and_basis(own, other, inverse, moved, counts):
    size = own.shape[1]
    blocks, rows, _ = moved.shape
    vmem = pl.BlockSpec(memory_space=pltpu.VMEM)
    return pl.pallas_call(
        core_kernel,
        out_shape=(
            jax.ShapeDtypeStruct((rows, size), F32),
            jax.ShapeDtypeStruct((128, size), BF16),
        ),
        in_specs=[vmem, vmem, vmem, vmem, pl.BlockSpec(memory_space=pltpu.SMEM)],
        out_specs=(vmem, vmem),
        scratch_shapes=[pltpu.VMEM((blocks, rows // 8, 8, size), F32)],
        name="core",
    )(own, other, inverse, moved, counts)


def local(tensor_slabs, slab_counts, column_scale, samples):
    rows, slots, width = tensor_slabs.shape
    sketch = samples.shape[1]
    blocks = lax.axis_size("gx")
    members = lax.axis_size("yz")
    chips = members // 2
    swap = [(j, j ^ 1) for j in range(members)]
    same_core = [[2 * y + c for y in range(chips)] for c in range(2)]
    keep, send, chunks = sketch_parts(tensor_slabs, slab_counts, column_scale, samples)
    half = keep + lax.ppermute(send, "yz", swap)
    parts = lax.all_to_all(
        half.reshape(chips, -1, sketch), "yz", 0, 0, axis_index_groups=same_core, tiled=True
    )
    part = parts.sum(0)
    column = lax.all_to_all(jnp.broadcast_to(part, (blocks, *part.shape)), "gx", 0, 0, tiled=True)
    column = column.reshape(-1, sketch)
    own = lax.all_to_all(
        jnp.broadcast_to(column, (chips, *column.shape)), "yz", 0, 0,
        axis_index_groups=same_core, tiled=True,
    ).reshape(-1, sketch)
    other = lax.ppermute(own, "yz", swap)
    own, other, chunks = lax.optimization_barrier((own, other, chunks))
    moved = lax.all_to_all(chunks, "gx", 0, 0, tiled=True)
    inverse = inverse_factor(own, other)
    basis, core = core_and_basis(own, other, inverse, moved, slab_counts)
    core = jnp.moveaxis(core.reshape(slots, -1, sketch), 2, 0)
    return basis, core


def solution(mesh):
    placed = (P("gx", "yz", None), P(), P(), P())
    return jax.shard_map(
        local,
        mesh=mesh,
        in_specs=placed,
        out_specs=(P("gx", None), P(None, "yz", "gx")),
        check_vma=False,
    )
```

```python
import jax
import jax.numpy as jnp
from jax import lax
from jax.experimental import pallas as pl
from jax.experimental.pallas import tpu as pltpu
from jax.sharding import PartitionSpec as P


F32, BF16, I32 = jnp.float32, jnp.bfloat16, jnp.int32
NN, NT, TN = ((1,), (0,)), ((1,), (1,)), ((0,), (0,))
HIGHEST = lax.Precision.HIGHEST
AHEAD = 10
BLOCK = 64
STEPS = (0, 2, 1, 3)


def dot(a, b, dims, precision=None):
    return lax.dot_general(
        a, b, (dims, ((), ())), precision=precision, preferred_element_type=F32
    )


def signs(rows, picked):
    both = lax.broadcasted_iota(I32, (rows, picked.shape[1]), 0) & picked
    both = both ^ (both >> 4)
    both = both ^ (both >> 2)
    both = both ^ (both >> 1)
    return (1 - 2 * (both & 1)).astype(F32)


def own_slabs(counts_ref, index, groups):
    offset = jnp.int32(0)
    for group in range(groups):
        offset = offset + jnp.where(group < index, counts_ref[group], 0)
    return offset, counts_ref[index]


def sketch_kernel(tensor_ref, counts_ref, scale_ref, samples_ref, keep_ref, send_ref, moved_ref,
                  hadamard_ref, total_ref):
    rows, slots, width = tensor_ref.shape
    total_slabs, sketch = samples_ref.shape
    index = lax.axis_index("yz")
    offset, count = own_slabs(counts_ref, index, counts_ref.shape[0])
    lines = tensor_ref[...].astype(F32).reshape(rows * slots, width).astype(BF16)
    at = lax.broadcasted_iota(I32, (rows * slots, rows * slots), 0)
    of = lax.broadcasted_iota(I32, (rows * slots, rows * slots), 1)
    pick = ((at % rows) * slots + at // rows == of).astype(F32).astype(BF16)
    by_slot = dot(pick, lines, NN)
    total = jnp.zeros((rows, sketch), F32)
    for slot in range(slots):
        slab = jnp.minimum(offset + slot, total_slabs - 1)
        picked = samples_ref[pl.ds(slab, 1), :]
        low = signs(32, picked & 31)
        high = signs(width // 32, picked >> 5)
        for part in range(width // 32):
            hadamard_ref[slot, pl.ds(part * 32, 32), :] = (low * high[part : part + 1, :]).astype(BF16)
        piece = by_slot[slot * rows : (slot + 1) * rows]
        scaled = (piece * scale_ref[pl.ds(slab, 1), :]).astype(BF16)
        term = dot(scaled, hadamard_ref[slot], NN)
        total = total + jnp.where(slot < count, term, 0.0)
    total_ref[...] = total * (1.0 / (total_slabs * width) ** 0.5)
    core = index % 2
    half = rows // 2
    keep_ref[...] = total_ref[pl.ds(pl.multiple_of(core * half, half), half), :]
    send_ref[...] = total_ref[pl.ds(pl.multiple_of((1 - core) * half, half), half), :]
    chunk = 128 // slots
    for chunk_index in range(width // chunk):
        start = chunk_index * chunk
        moved_ref[chunk_index] = jnp.concatenate(
            [by_slot[s * rows : (s + 1) * rows, start : start + chunk] for s in range(slots)], axis=1
        ).astype(BF16)


def sketch_parts(tensor, counts, scale, samples):
    rows, slots, width = tensor.shape
    sketch = samples.shape[1]
    chunks = width * slots // 128
    vmem = pl.BlockSpec(memory_space=pltpu.VMEM)
    half = jax.ShapeDtypeStruct((rows // 2, sketch), F32)
    return pl.pallas_call(
        sketch_kernel,
        out_shape=(half, half, jax.ShapeDtypeStruct((chunks, rows, 128), BF16)),
        in_specs=[vmem, pl.BlockSpec(memory_space=pltpu.SMEM), vmem, vmem],
        out_specs=(vmem, vmem, vmem),
        scratch_shapes=[pltpu.VMEM((slots, width, sketch), BF16), pltpu.VMEM((rows, sketch), F32)],
        name="sketch",
    )(tensor, counts, scale, samples)


def block_inverse(tiles):
    count = len(tiles)
    size = 8 * count
    lines = list(tiles)
    sub = lax.broadcasted_iota(I32, (8, 128), 0)
    lane = lax.broadcasted_iota(I32, (8, 128), 1)

    def row_of(tile, at):
        return jnp.broadcast_to(tile[at : at + 1, :], (8, 128))

    def column_of(tile, at):
        return jnp.broadcast_to(tile[:, at : at + 1], (8, 128))

    columns = {j: [column_of(tile, j) for tile in lines] for j in range(min(AHEAD, size))}
    pivots = [jnp.ones((8, 128), F32)] * count
    for step in range(size):
        tile, at = divmod(step, 8)
        column = columns.pop(step)
        pivot = row_of(column[tile], at)
        pivots[tile] = jnp.where(sub == at, pivot, pivots[tile])
        if step == size - 1:
            break
        inverse = 1.0 / pivot
        factors = {t: column[t] * inverse for t in range(tile, count)}
        factors[tile] = jnp.where(sub > at, factors[tile], 0.0)
        if at == 7:
            factors.pop(tile)
        for later in columns.values():
            value = row_of(later[tile], at)
            for t, factor in factors.items():
                later[t] = later[t] - factor * value
        line = jnp.where(lane == step, 1.0, row_of(lines[tile], at))
        for t, factor in factors.items():
            cleared = (lane == step) if t > tile else (lane == step) & (sub > at)
            lines[t] = jnp.where(cleared, 0.0, lines[t]) - factor * line
        new = step + AHEAD
        if new < size:
            columns[new] = [
                column_of(lines[t], new) if t >= (step + 1) // 8 else None for t in range(count)
            ]
    result = []
    for t in range(count):
        inside = jnp.where(lane == sub + 8 * t, 1.0, 0.0)
        result.append(lax.rsqrt(pivots[t]) * jnp.where(lane < sub + 8 * t, lines[t], inside))
    return jnp.concatenate(result, 0)


def invert_factor(work_ref):
    size = work_ref.shape[0]
    lanes = lax.broadcasted_iota(I32, (1, size), 1)

    def spread(block):
        return jnp.concatenate([block, jnp.zeros((BLOCK, 128 - BLOCK), F32)], 1)

    diagonal = spread(work_ref[0:BLOCK, 0:BLOCK])
    for start in range(0, size, BLOCK):
        end = start + BLOCK
        after = end + BLOCK
        inverse = block_inverse([diagonal[8 * t : 8 * t + 8] for t in range(BLOCK // 8)])[:, :BLOCK]
        if end < size:
            below = dot(work_ref[end:after, start:end], inverse, NT, HIGHEST)
            diagonal = spread(work_ref[end:after, end:after] - dot(below, below, NT, HIGHEST))
            rest = dot(work_ref[end:, start:end], inverse, NT, HIGHEST)
        work_ref[start:end, :] = dot(inverse, work_ref[start:end, :], NN, HIGHEST)
        work_ref[start:end, start:end] = inverse
        if end < size:
            here = (lanes >= start) & (lanes < end)
            work_ref[end:, :] = jnp.where(here, 0.0, work_ref[end:, :]) - dot(
                rest, work_ref[start:end, :], NN, HIGHEST
            )
    row = lax.broadcasted_iota(I32, (size, size), 0)
    column = lax.broadcasted_iota(I32, (size, size), 1)
    work_ref[...] = jnp.where(row >= column, work_ref[...], 0.0)


def halves(array):
    high = array.astype(BF16)
    return high, (array - high.astype(F32)).astype(BF16)


def finish_kernel(*refs):
    sources, (counts_ref, basis_ref, core_ref), scratch = refs[:9], refs[9:12], refs[12:]
    work_ref, rows_ref, sems = scratch
    blocks, parts, line, size = rows_ref.shape
    chips = parts // 2
    index = lax.axis_index("yz")
    core, chip = index % 2, index // 2
    places = [
        which * chips + (chip + chips - step) % chips for which in (core, 1 - core) for step in STEPS
    ]
    copies = [
        pltpu.make_async_copy(source, rows_ref.at[:, place], sems.at[number])
        for number, (source, place) in enumerate(zip(sources[:8], places))
    ]
    for copy in copies:
        copy.start()
    gram = jnp.zeros((size, size), F32)
    for source in sources[:8]:
        piece = source[...].reshape(blocks * line, size)
        gram = gram + dot(piece, piece, TN, HIGHEST)
    work_ref[...] = gram
    invert_factor(work_ref)
    for copy in copies:
        copy.wait()
    inverse = work_ref[...]
    inverse_high, inverse_low = halves(inverse)
    block = rows_ref[lax.axis_index("gx")].reshape(parts * line, size)
    basis_ref[...] = dot(block, inverse, NT, HIGHEST)
    high, low = halves(rows_ref[...].reshape(blocks * parts * line, size))
    every = dot(high, inverse_high, NT) + dot(high, inverse_low, NT) + dot(low, inverse_high, NT)
    result = dot(sources[8][...].reshape(blocks * parts * line, 128), every.astype(BF16), TN)
    slots = 4
    slot = lax.broadcasted_iota(I32, result.shape, 0) // (128 // slots)
    core_ref[...] = jnp.where(slot < counts_ref[index], result, 0.0).astype(BF16)


def finish(pieces, moved, counts):
    blocks, rows, _ = moved.shape
    line, size = pieces[0].shape[1:]
    vmem = pl.BlockSpec(memory_space=pltpu.VMEM)
    return pl.pallas_call(
        finish_kernel,
        out_shape=(
            jax.ShapeDtypeStruct((rows, size), F32),
            jax.ShapeDtypeStruct((128, size), BF16),
        ),
        in_specs=[vmem] * 9 + [pl.BlockSpec(memory_space=pltpu.SMEM)],
        out_specs=(vmem, vmem),
        scratch_shapes=[
            pltpu.VMEM((size, size), F32),
            pltpu.VMEM((blocks, rows // line, line, size), F32),
            pltpu.SemaphoreType.DMA((8,)),
        ],
        name="finish",
    )(*(pltpu.with_memory_space_constraint(each, pltpu.VMEM) for each in (*pieces, moved)), counts)


def local(tensor_slabs, slab_counts, column_scale, samples):
    _, slots, _ = tensor_slabs.shape
    sketch = samples.shape[1]
    blocks = lax.axis_size("gx")
    members = lax.axis_size("yz")
    chips = members // 2
    swap = [(j, j ^ 1) for j in range(members)]
    same_core = [[2 * y + c for y in range(chips)] for c in range(2)]
    keep, send, chunks = sketch_parts(tensor_slabs, slab_counts, column_scale, samples)
    half = keep + lax.ppermute(send, "yz", swap)
    parts = lax.all_to_all(
        half.reshape(chips, -1, sketch), "yz", 0, 0, axis_index_groups=same_core, tiled=True
    )
    part = jnp.broadcast_to(parts.sum(0), (blocks, *parts.shape[1:]))
    column = lax.all_to_all(part, "gx", 0, 0, tiled=True)
    pieces = [column]
    for step in STEPS[1:]:
        turn = [(j, (j + 2 * step) % members) for j in range(members)]
        pieces.append(lax.ppermute(column, "yz", turn))
    moved = lax.all_to_all(chunks, "gx", 0, 0, tiled=True)
    live = jnp.minimum(slab_counts, slots)
    pieces = pieces + [lax.ppermute(piece, "yz", swap) for piece in pieces]
    basis, core = finish(pieces, moved, live)
    core = jnp.moveaxis(core.reshape(slots, -1, sketch), 2, 0)
    return basis, core


def solution(mesh):
    placed = (P("gx", "yz", None), P(), P(), P())
    return jax.shard_map(
        local,
        mesh=mesh,
        in_specs=placed,
        out_specs=(P("gx", None), P(None, "yz", "gx")),
        check_vma=False,
    )
```

```python
import jax
import jax.numpy as jnp
from jax import lax
from jax.experimental import pallas as pl
from jax.experimental.pallas import tpu as pltpu
from jax.sharding import PartitionSpec as P


F32, BF16, I32 = jnp.float32, jnp.bfloat16, jnp.int32
NN, NT, TN = ((1,), (0,)), ((1,), (1,)), ((0,), (0,))
HIGHEST = lax.Precision.HIGHEST
AHEAD = 10
BLOCK = 64
STEPS = (0, 2, 1, 3)
SLOTS = 4
ROOM = pltpu.CompilerParams(vmem_limit_bytes=24 << 20)


def dot(a, b, dims, precision=None):
    return lax.dot_general(
        a, b, (dims, ((), ())), precision=precision, preferred_element_type=F32
    )


def signs(rows, picked):
    both = lax.broadcasted_iota(I32, (rows, picked.shape[1]), 0) & picked
    both = both ^ (both >> 4)
    both = both ^ (both >> 2)
    both = both ^ (both >> 1)
    return (1 - 2 * (both & 1)).astype(F32)


def own_slabs(counts_ref, index, groups):
    offset = jnp.int32(0)
    for group in range(groups):
        offset = offset + jnp.where(group < index, counts_ref[group], 0)
    return offset, counts_ref[index]


def sketch_kernel(tensor_ref, counts_ref, scale_ref, samples_ref, total_ref, moved_ref, hadamard_ref):
    rows, slots, width = tensor_ref.shape
    total_slabs, sketch = samples_ref.shape
    index = lax.axis_index("yz")
    offset, count = own_slabs(counts_ref, index, counts_ref.shape[0])
    lines = tensor_ref[...].astype(F32).reshape(rows * slots, width).astype(BF16)
    at = lax.broadcasted_iota(I32, (rows * slots, rows * slots), 0)
    of = lax.broadcasted_iota(I32, (rows * slots, rows * slots), 1)
    pick = ((at % rows) * slots + at // rows == of).astype(F32).astype(BF16)
    by_slot = dot(pick, lines, NN)
    total = jnp.zeros((rows, sketch), F32)
    for slot in range(slots):
        slab = jnp.minimum(offset + slot, total_slabs - 1)
        picked = samples_ref[pl.ds(slab, 1), :]
        low = signs(32, picked & 31)
        high = signs(width // 32, picked >> 5)
        for part in range(width // 32):
            hadamard_ref[slot, pl.ds(part * 32, 32), :] = (low * high[part : part + 1, :]).astype(BF16)
        piece = by_slot[slot * rows : (slot + 1) * rows]
        scaled = (piece * scale_ref[pl.ds(slab, 1), :]).astype(BF16)
        term = dot(scaled, hadamard_ref[slot], NN)
        total = total + jnp.where(slot < count, term, 0.0)
    total_ref[...] = total * (1.0 / (total_slabs * width) ** 0.5)
    chunk = 128 // slots
    for chunk_index in range(width // chunk):
        start = chunk_index * chunk
        moved_ref[chunk_index] = jnp.concatenate(
            [by_slot[s * rows : (s + 1) * rows, start : start + chunk] for s in range(slots)], axis=1
        ).astype(BF16)


def sketch_parts(tensor, counts, scale, samples):
    rows, slots, width = tensor.shape
    sketch = samples.shape[1]
    chunks = width * slots // 128
    vmem = pl.BlockSpec(memory_space=pltpu.VMEM)
    return pl.pallas_call(
        sketch_kernel,
        out_shape=(pltpu.VMEM((rows, sketch), F32), pltpu.VMEM((chunks, rows, 128), BF16)),
        in_specs=[vmem, pl.BlockSpec(memory_space=pltpu.SMEM), vmem, vmem],
        out_specs=(vmem, vmem),
        scratch_shapes=[pltpu.VMEM((slots, width, sketch), BF16)],
        name="sketch",
    )(tensor, counts, scale, samples)


def block_inverse(tiles):
    count = len(tiles)
    size = 8 * count
    lines = list(tiles)
    sub = lax.broadcasted_iota(I32, (8, 128), 0)
    lane = lax.broadcasted_iota(I32, (8, 128), 1)

    def row_of(tile, at):
        return jnp.broadcast_to(tile[at : at + 1, :], (8, 128))

    def column_of(tile, at):
        return jnp.broadcast_to(tile[:, at : at + 1], (8, 128))

    columns = {j: [column_of(tile, j) for tile in lines] for j in range(min(AHEAD, size))}
    pivots = [jnp.ones((8, 128), F32)] * count
    for step in range(size):
        tile, at = divmod(step, 8)
        column = columns.pop(step)
        pivot = row_of(column[tile], at)
        pivots[tile] = jnp.where(sub == at, pivot, pivots[tile])
        if step == size - 1:
            break
        inverse = 1.0 / pivot
        factors = {t: column[t] * inverse for t in range(tile, count)}
        factors[tile] = jnp.where(sub > at, factors[tile], 0.0)
        if at == 7:
            factors.pop(tile)
        for later in columns.values():
            value = row_of(later[tile], at)
            for t, factor in factors.items():
                later[t] = later[t] - factor * value
        line = jnp.where(lane == step, 1.0, row_of(lines[tile], at))
        for t, factor in factors.items():
            cleared = (lane == step) if t > tile else (lane == step) & (sub > at)
            lines[t] = jnp.where(cleared, 0.0, lines[t]) - factor * line
        new = step + AHEAD
        if new < size:
            columns[new] = [
                column_of(lines[t], new) if t >= (step + 1) // 8 else None for t in range(count)
            ]
    result = []
    for t in range(count):
        inside = jnp.where(lane == sub + 8 * t, 1.0, 0.0)
        result.append(lax.rsqrt(pivots[t]) * jnp.where(lane < sub + 8 * t, lines[t], inside))
    return jnp.concatenate(result, 0)


def invert_factor(work_ref):
    size = work_ref.shape[0]
    lanes = lax.broadcasted_iota(I32, (1, size), 1)

    def spread(block):
        return jnp.concatenate([block, jnp.zeros((BLOCK, 128 - BLOCK), F32)], 1)

    diagonal = spread(work_ref[0:BLOCK, 0:BLOCK])
    for start in range(0, size, BLOCK):
        end = start + BLOCK
        after = end + BLOCK
        inverse = block_inverse([diagonal[8 * t : 8 * t + 8] for t in range(BLOCK // 8)])[:, :BLOCK]
        if end < size:
            below = dot(work_ref[end:after, start:end], inverse, NT, HIGHEST)
            diagonal = spread(work_ref[end:after, end:after] - dot(below, below, NT, HIGHEST))
            rest = dot(work_ref[end:, start:end], inverse, NT, HIGHEST)
        work_ref[start:end, :] = dot(inverse, work_ref[start:end, :], NN, HIGHEST)
        work_ref[start:end, start:end] = inverse
        if end < size:
            here = (lanes >= start) & (lanes < end)
            work_ref[end:, :] = jnp.where(here, 0.0, work_ref[end:, :]) - dot(
                rest, work_ref[start:end, :], NN, HIGHEST
            )
    row = lax.broadcasted_iota(I32, (size, size), 0)
    column = lax.broadcasted_iota(I32, (size, size), 1)
    work_ref[...] = jnp.where(row >= column, work_ref[...], 0.0)


def halves(array):
    high = array.astype(BF16)
    return high, (array - high.astype(F32)).astype(BF16)


def gram_of(pieces):
    total = None
    for piece in pieces:
        flat = piece[...].reshape(-1, piece.shape[-1])
        term = dot(flat, flat, TN, HIGHEST)
        total = term if total is None else total + term
    return total


def gram_kernel(*refs):
    refs[-1][...] = gram_of(refs[:-1])


def factor_kernel(*refs):
    pieces, gram_ref, (work_ref, rows_ref, sems) = refs[:8], refs[8], refs[9:]
    members = len(pieces)
    index = lax.axis_index("yz")
    core, chip = index % 2, index // 2
    chips = members // 2
    copies = []
    for number, piece in enumerate(pieces):
        which, step = divmod(number, chips)
        place = 2 * ((chip + chips - STEPS[step]) % chips) + (core if which == 0 else 1 - core)
        copies.append(pltpu.make_async_copy(piece, rows_ref.at[:, place], sems.at[number]))
        copies[-1].start()
    work_ref[...] = gram_ref[...] + gram_of(
        [piece for number, piece in enumerate(pieces) if number % chips]
    )
    invert_factor(work_ref)
    for copy in copies:
        copy.wait()


def core_kernel(rows_ref, inverse_ref, moved_ref, counts_ref, basis_ref, core_ref):
    blocks, parts, line, size = rows_ref.shape
    inverse = inverse_ref[...]
    inverse_high, inverse_low = halves(inverse)
    block = rows_ref[lax.axis_index("gx")].reshape(parts * line, size)
    basis_ref[...] = dot(block, inverse, NT, HIGHEST)
    high, low = halves(rows_ref[...].reshape(blocks * parts * line, size))
    every = dot(high, inverse_high, NT) + dot(high, inverse_low, NT) + dot(low, inverse_high, NT)
    result = dot(moved_ref[...].reshape(blocks * parts * line, 128), every.astype(BF16), TN)
    slot = lax.broadcasted_iota(I32, result.shape, 0) // (128 // SLOTS)
    live = slot < counts_ref[lax.axis_index("yz")]
    core_ref[...] = jnp.where(live, result, 0.0).astype(BF16)


def near(*arrays):
    return tuple(pltpu.with_memory_space_constraint(each, pltpu.VMEM) for each in arrays)


def gram_part(*pieces):
    size = pieces[0].shape[-1]
    vmem = pl.BlockSpec(memory_space=pltpu.VMEM)
    return pl.pallas_call(
        gram_kernel,
        out_shape=pltpu.VMEM((size, size), F32),
        in_specs=[vmem] * len(pieces),
        out_specs=vmem,
        name="gram",
        compiler_params=ROOM,
    )(*near(*pieces))


def inverse_factor(pieces, gram):
    blocks, line, size = pieces[0].shape
    vmem = pl.BlockSpec(memory_space=pltpu.VMEM)
    return pl.pallas_call(
        factor_kernel,
        out_shape=(
            jax.ShapeDtypeStruct((size, size), F32),
            pltpu.VMEM((blocks, len(pieces), line, size), F32),
        ),
        in_specs=[vmem if number % len(STEPS) else pl.BlockSpec(memory_space=pl.ANY) for number in range(8)]
        + [vmem],
        out_specs=(vmem, vmem),
        scratch_shapes=[pltpu.SemaphoreType.DMA((8,))],
        name="factor",
        compiler_params=ROOM,
    )(*(near(piece)[0] if number % len(STEPS) else piece for number, piece in enumerate(pieces)), *near(gram))


def core_and_basis(every, inverse, moved, counts):
    _, parts, line, size = every.shape
    vmem = pl.BlockSpec(memory_space=pltpu.VMEM)
    return pl.pallas_call(
        core_kernel,
        out_shape=(
            jax.ShapeDtypeStruct((parts * line, size), F32),
            jax.ShapeDtypeStruct((128, size), BF16),
        ),
        in_specs=[vmem, vmem, vmem, pl.BlockSpec(memory_space=pltpu.SMEM)],
        out_specs=(vmem, vmem),
        name="core",
        compiler_params=ROOM,
    )(*near(every), inverse, *near(moved), counts)


def local(tensor_slabs, slab_counts, column_scale, samples):
    _, slots, _ = tensor_slabs.shape
    sketch = samples.shape[1]
    blocks = lax.axis_size("gx")
    members = lax.axis_size("yz")
    swap = [(j, j ^ 1) for j in range(members)]
    total, chunks = sketch_parts(tensor_slabs, slab_counts, column_scale, samples)
    parts = lax.all_to_all(total.reshape(members, -1, sketch), "yz", 0, 0, tiled=True)
    part = jnp.broadcast_to(parts.sum(0), (blocks, *parts.shape[1:]))
    column = lax.all_to_all(part, "gx", 0, 0, tiled=True)
    pieces = [column]
    for step in STEPS[1:]:
        turn = [(j, (j + 2 * step) % members) for j in range(members)]
        pieces.append(lax.ppermute(column, "yz", turn))
    moved = lax.all_to_all(chunks, "gx", 0, 0, tiled=True)
    live = jnp.minimum(slab_counts, slots)
    pieces = pieces + [lax.ppermute(piece, "yz", swap) for piece in pieces]
    gram = gram_part(pieces[0], pieces[len(STEPS)])
    inverse, every = inverse_factor(pieces, gram)
    basis, core = core_and_basis(every, inverse, moved, live)
    core = jnp.moveaxis(core.reshape(slots, -1, sketch), 2, 0)
    return basis, core


def solution(mesh):
    placed = (P("gx", "yz", None), P(), P(), P())
    return jax.shard_map(
        local,
        mesh=mesh,
        in_specs=placed,
        out_specs=(P("gx", None), P(None, "yz", "gx")),
        check_vma=False,
    )
```

```python
import jax
import jax.numpy as jnp
from jax import lax
from jax.experimental import pallas as pl
from jax.experimental.pallas import tpu as pltpu
from jax.sharding import PartitionSpec as P


F32, BF16, I32 = jnp.float32, jnp.bfloat16, jnp.int32
NN, NT, TN = ((1,), (0,)), ((1,), (1,)), ((0,), (0,))
HIGHEST = lax.Precision.HIGHEST
AHEAD = 10
BLOCK = 64
STEPS = (0, 2, 1, 3)
SLOTS = 4
SHARES = 4
ROOM = pltpu.CompilerParams(vmem_limit_bytes=24 << 20)


def dot(a, b, dims, precision=None):
    return lax.dot_general(
        a, b, (dims, ((), ())), precision=precision, preferred_element_type=F32
    )


def signs(rows, picked):
    both = lax.broadcasted_iota(I32, (rows, picked.shape[1]), 0) & picked
    both = both ^ (both >> 4)
    both = both ^ (both >> 2)
    both = both ^ (both >> 1)
    return (1 - 2 * (both & 1)).astype(F32)


def own_slabs(counts_ref, index, groups):
    offset = jnp.int32(0)
    for group in range(groups):
        offset = offset + jnp.where(group < index, counts_ref[group], 0)
    return offset, counts_ref[index]


def sketch_kernel(tensor_ref, counts_ref, scale_ref, samples_ref, total_ref, moved_ref, hadamard_ref):
    rows, slots, width = tensor_ref.shape
    total_slabs, sketch = samples_ref.shape
    index = lax.axis_index("yz")
    offset, count = own_slabs(counts_ref, index, counts_ref.shape[0])
    lines = tensor_ref[...].astype(F32).reshape(rows * slots, width).astype(BF16)
    at = lax.broadcasted_iota(I32, (rows * slots, rows * slots), 0)
    of = lax.broadcasted_iota(I32, (rows * slots, rows * slots), 1)
    pick = ((at % rows) * slots + at // rows == of).astype(F32).astype(BF16)
    by_slot = dot(pick, lines, NN)
    total = jnp.zeros((rows, sketch), F32)
    for slot in range(slots):
        slab = jnp.minimum(offset + slot, total_slabs - 1)
        picked = samples_ref[pl.ds(slab, 1), :]
        low = signs(32, picked & 31)
        high = signs(width // 32, picked >> 5)
        for part in range(width // 32):
            hadamard_ref[slot, pl.ds(part * 32, 32), :] = (low * high[part : part + 1, :]).astype(BF16)
        piece = by_slot[slot * rows : (slot + 1) * rows]
        scaled = (piece * scale_ref[pl.ds(slab, 1), :]).astype(BF16)
        term = dot(scaled, hadamard_ref[slot], NN)
        total = total + jnp.where(slot < count, term, 0.0)
    total_ref[...] = total * (1.0 / (total_slabs * width) ** 0.5)
    chunk = 128 // slots
    for chunk_index in range(width // chunk):
        start = chunk_index * chunk
        moved_ref[chunk_index] = jnp.concatenate(
            [by_slot[s * rows : (s + 1) * rows, start : start + chunk] for s in range(slots)], axis=1
        ).astype(BF16)


def sketch_parts(tensor, counts, scale, samples):
    rows, slots, width = tensor.shape
    sketch = samples.shape[1]
    chunks = width * slots // 128
    vmem = pl.BlockSpec(memory_space=pltpu.VMEM)
    return pl.pallas_call(
        sketch_kernel,
        out_shape=(pltpu.VMEM((rows, sketch), F32), jax.ShapeDtypeStruct((chunks, rows, 128), BF16)),
        in_specs=[vmem, pl.BlockSpec(memory_space=pltpu.SMEM), vmem, vmem],
        out_specs=(vmem, vmem),
        scratch_shapes=[pltpu.VMEM((slots, width, sketch), BF16)],
        name="sketch",
    )(tensor, counts, scale, samples)


def block_inverse(tiles):
    count = len(tiles)
    size = 8 * count
    lines = list(tiles)
    sub = lax.broadcasted_iota(I32, (8, 128), 0)
    lane = lax.broadcasted_iota(I32, (8, 128), 1)

    def row_of(tile, at):
        return jnp.broadcast_to(tile[at : at + 1, :], (8, 128))

    def column_of(tile, at):
        return jnp.broadcast_to(tile[:, at : at + 1], (8, 128))

    columns = {j: [column_of(tile, j) for tile in lines] for j in range(min(AHEAD, size))}
    pivots = [jnp.ones((8, 128), F32)] * count
    for step in range(size):
        tile, at = divmod(step, 8)
        column = columns.pop(step)
        pivot = row_of(column[tile], at)
        pivots[tile] = jnp.where(sub == at, pivot, pivots[tile])
        if step == size - 1:
            break
        inverse = 1.0 / pivot
        factors = {t: column[t] * inverse for t in range(tile, count)}
        factors[tile] = jnp.where(sub > at, factors[tile], 0.0)
        if at == 7:
            factors.pop(tile)
        for later in columns.values():
            value = row_of(later[tile], at)
            for t, factor in factors.items():
                later[t] = later[t] - factor * value
        line = jnp.where(lane == step, 1.0, row_of(lines[tile], at))
        for t, factor in factors.items():
            cleared = (lane == step) if t > tile else (lane == step) & (sub > at)
            lines[t] = jnp.where(cleared, 0.0, lines[t]) - factor * line
        new = step + AHEAD
        if new < size:
            columns[new] = [
                column_of(lines[t], new) if t >= (step + 1) // 8 else None for t in range(count)
            ]
    result = []
    for t in range(count):
        inside = jnp.where(lane == sub + 8 * t, 1.0, 0.0)
        result.append(lax.rsqrt(pivots[t]) * jnp.where(lane < sub + 8 * t, lines[t], inside))
    return jnp.concatenate(result, 0)


def invert_factor(work_ref):
    size = work_ref.shape[0]
    lanes = lax.broadcasted_iota(I32, (1, size), 1)

    def spread(block):
        return jnp.concatenate([block, jnp.zeros((BLOCK, 128 - BLOCK), F32)], 1)

    diagonal = spread(work_ref[0:BLOCK, 0:BLOCK])
    for start in range(0, size, BLOCK):
        end = start + BLOCK
        after = end + BLOCK
        inverse = block_inverse([diagonal[8 * t : 8 * t + 8] for t in range(BLOCK // 8)])[:, :BLOCK]
        if end < size:
            below = dot(work_ref[end:after, start:end], inverse, NT, HIGHEST)
            diagonal = spread(work_ref[end:after, end:after] - dot(below, below, NT, HIGHEST))
            rest = dot(work_ref[end:, start:end], inverse, NT, HIGHEST)
        work_ref[start:end, :] = dot(inverse, work_ref[start:end, :], NN, HIGHEST)
        work_ref[start:end, start:end] = inverse
        if end < size:
            here = (lanes >= start) & (lanes < end)
            work_ref[end:, :] = jnp.where(here, 0.0, work_ref[end:, :]) - dot(
                rest, work_ref[start:end, :], NN, HIGHEST
            )
    row = lax.broadcasted_iota(I32, (size, size), 0)
    column = lax.broadcasted_iota(I32, (size, size), 1)
    work_ref[...] = jnp.where(row >= column, work_ref[...], 0.0)


def halves(array):
    high = array.astype(BF16)
    return high, (array - high.astype(F32)).astype(BF16)


def gram_of(pieces):
    square = cross = None
    for piece in pieces:
        flat = piece[...].reshape(-1, piece.shape[-1])
        high, rest = halves(flat)
        low = (flat - high.astype(F32) - rest.astype(F32)).astype(BF16)
        even = dot(high, high, TN) + dot(rest, rest, TN)
        odd = dot(high, rest, TN) + dot(high, low, TN)
        square = even if square is None else square + even
        cross = odd if cross is None else cross + odd
    return square + (cross + cross.T)


def gram_kernel(*refs):
    refs[-1][...] = gram_of(refs[:-1])


def factor_kernel(*refs):
    pieces, gram_ref, (work_ref, rows_ref, sems) = refs[:8], refs[8], refs[9:]
    members = len(pieces)
    index = lax.axis_index("yz")
    core, chip = index % 2, index // 2
    chips = members // 2
    copies = []
    for number, piece in enumerate(pieces):
        which, step = divmod(number, chips)
        place = 2 * ((chip + chips - STEPS[step]) % chips) + (core if which == 0 else 1 - core)
        copies.append(pltpu.make_async_copy(piece, rows_ref.at[:, place], sems.at[number]))
        copies[-1].start()
    work_ref[...] = gram_ref[...] + gram_of(
        [piece for number, piece in enumerate(pieces) if number % chips]
    )
    invert_factor(work_ref)
    for copy in copies:
        copy.wait()


def core_kernel(rows_any, inverse_ref, moved_any, counts_ref, basis_ref, core_ref,
                rows_ref, moved_ref, block_ref, sems):
    blocks, parts, line, size = rows_ref.shape
    share = blocks // SHARES
    own = pltpu.make_async_copy(rows_any.at[lax.axis_index("gx")], block_ref, sems.at[SHARES + 1])
    whole = pltpu.make_async_copy(moved_any, moved_ref, sems.at[SHARES])
    copies = []
    for number in range(SHARES):
        place = pl.ds(number * share, share)
        copies.append(
            pltpu.make_async_copy(rows_any.at[place], rows_ref.at[place], sems.at[number])
        )
    for copy in (own, *copies, whole):
        copy.start()
    inverse = inverse_ref[...]
    inverse_high, inverse_low = halves(inverse)
    own.wait()
    basis_ref[...] = dot(block_ref[...].reshape(parts * line, size), inverse, NT, HIGHEST)
    result = jnp.zeros((128, size), F32)
    for number, copy in enumerate(copies):
        copy.wait()
        place = slice(number * share, (number + 1) * share)
        high, low = halves(rows_ref[place].reshape(share * parts * line, size))
        every = dot(high, inverse_high, NT) + dot(high, inverse_low, NT) + dot(low, inverse_high, NT)
        if number == 0:
            whole.wait()
        result = result + dot(moved_ref[place].reshape(share * parts * line, 128), every.astype(BF16), TN)
    slot = lax.broadcasted_iota(I32, result.shape, 0) // (128 // SLOTS)
    live = slot < counts_ref[lax.axis_index("yz")]
    core_ref[...] = jnp.where(live, result, 0.0).astype(BF16)


def near(*arrays):
    return tuple(pltpu.with_memory_space_constraint(each, pltpu.VMEM) for each in arrays)


def gram_part(*pieces):
    size = pieces[0].shape[-1]
    vmem = pl.BlockSpec(memory_space=pltpu.VMEM)
    return pl.pallas_call(
        gram_kernel,
        out_shape=pltpu.VMEM((size, size), F32),
        in_specs=[vmem] * len(pieces),
        out_specs=vmem,
        name="gram",
        compiler_params=ROOM,
    )(*near(*pieces))


def inverse_factor(pieces, gram):
    blocks, line, size = pieces[0].shape
    vmem = pl.BlockSpec(memory_space=pltpu.VMEM)
    return pl.pallas_call(
        factor_kernel,
        out_shape=(
            pltpu.HBM((size, size), F32),
            pltpu.HBM((blocks, len(pieces), line, size), F32),
        ),
        in_specs=[vmem if number % len(STEPS) else pl.BlockSpec(memory_space=pl.ANY) for number in range(8)]
        + [vmem],
        out_specs=(vmem, pl.BlockSpec(memory_space=pl.ANY)),
        scratch_shapes=[pltpu.SemaphoreType.DMA((8,))],
        name="factor",
        compiler_params=ROOM,
    )(*(near(piece)[0] if number % len(STEPS) else piece for number, piece in enumerate(pieces)), *near(gram))


def core_and_basis(every, inverse, moved, counts):
    _, parts, line, size = every.shape
    vmem = pl.BlockSpec(memory_space=pltpu.VMEM)
    free = pl.BlockSpec(memory_space=pl.ANY)
    return pl.pallas_call(
        core_kernel,
        out_shape=(
            jax.ShapeDtypeStruct((parts * line, size), F32),
            jax.ShapeDtypeStruct((128, size), BF16),
        ),
        in_specs=[free, vmem, free, pl.BlockSpec(memory_space=pltpu.SMEM)],
        out_specs=(vmem, vmem),
        scratch_shapes=[
            pltpu.VMEM(every.shape, F32),
            pltpu.VMEM(moved.shape, BF16),
            pltpu.VMEM((parts, line, size), F32),
            pltpu.SemaphoreType.DMA((SHARES + 2,)),
        ],
        name="core",
        compiler_params=ROOM,
    )(*(pltpu.with_memory_space_constraint(each, pltpu.HBM) for each in (every, inverse)), moved, counts)


def local(tensor_slabs, slab_counts, column_scale, samples):
    _, slots, _ = tensor_slabs.shape
    sketch = samples.shape[1]
    blocks = lax.axis_size("gx")
    members = lax.axis_size("yz")
    swap = [(j, j ^ 1) for j in range(members)]
    total, chunks = sketch_parts(tensor_slabs, slab_counts, column_scale, samples)
    parts = lax.all_to_all(total.reshape(members, -1, sketch), "yz", 0, 0, tiled=True)
    part = jnp.broadcast_to(parts.sum(0), (blocks, *parts.shape[1:]))
    column = lax.all_to_all(part, "gx", 0, 0, tiled=True)
    pieces = [column]
    for step in STEPS[1:]:
        turn = [(j, (j + 2 * step) % members) for j in range(members)]
        pieces.append(lax.ppermute(column, "yz", turn))
    moved = lax.all_to_all(chunks, "gx", 0, 0, tiled=True)
    live = jnp.minimum(slab_counts, slots)
    pieces = pieces + [lax.ppermute(piece, "yz", swap) for piece in pieces]
    gram = gram_part(pieces[0], pieces[len(STEPS)])
    inverse, every = inverse_factor(pieces, gram)
    basis, core = core_and_basis(every, inverse, moved, live)
    core = jnp.moveaxis(core.reshape(slots, -1, sketch), 2, 0)
    return basis, core


def solution(mesh):
    placed = (P("gx", "yz", None), P(), P(), P())
    return jax.shard_map(
        local,
        mesh=mesh,
        in_specs=placed,
        out_specs=(P("gx", None), P(None, "yz", "gx")),
        check_vma=False,
    )
```

```python
import jax
import jax.numpy as jnp
from jax import lax
from jax.experimental import pallas as pl
from jax.experimental.pallas import tpu as pltpu
from jax.sharding import PartitionSpec as P


F32, BF16, I32 = jnp.float32, jnp.bfloat16, jnp.int32
NN, NT, TN = ((1,), (0,)), ((1,), (1,)), ((0,), (0,))
HIGHEST = lax.Precision.HIGHEST
AHEAD = 10
BLOCK = 64
STEPS = (0, 2, 1, 3)
SLOTS = 4
ROOM = pltpu.CompilerParams(vmem_limit_bytes=24 << 20)


def dot(a, b, dims, precision=None):
    return lax.dot_general(
        a, b, (dims, ((), ())), precision=precision, preferred_element_type=F32
    )


def signs(rows, picked):
    both = lax.broadcasted_iota(I32, (rows, picked.shape[1]), 0) & picked
    both = both ^ (both >> 4)
    both = both ^ (both >> 2)
    both = both ^ (both >> 1)
    return (1 - 2 * (both & 1)).astype(F32)


def own_slabs(counts_ref, index, groups):
    offset = jnp.int32(0)
    for group in range(groups):
        offset = offset + jnp.where(group < index, counts_ref[group], 0)
    return offset, counts_ref[index]


def sketch_kernel(tensor_ref, counts_ref, scale_ref, samples_ref, total_ref, moved_ref, hadamard_ref):
    rows, slots, width = tensor_ref.shape
    total_slabs, sketch = samples_ref.shape
    index = lax.axis_index("yz")
    offset, count = own_slabs(counts_ref, index, counts_ref.shape[0])
    lines = tensor_ref[...].astype(F32).reshape(rows * slots, width).astype(BF16)
    at = lax.broadcasted_iota(I32, (rows * slots, rows * slots), 0)
    of = lax.broadcasted_iota(I32, (rows * slots, rows * slots), 1)
    pick = ((at % rows) * slots + at // rows == of).astype(F32).astype(BF16)
    by_slot = dot(pick, lines, NN)
    total = jnp.zeros((rows, sketch), F32)
    for slot in range(slots):
        slab = jnp.minimum(offset + slot, total_slabs - 1)
        picked = samples_ref[pl.ds(slab, 1), :]
        low = signs(32, picked & 31)
        high = signs(width // 32, picked >> 5)
        for part in range(width // 32):
            hadamard_ref[slot, pl.ds(part * 32, 32), :] = (low * high[part : part + 1, :]).astype(BF16)
        piece = by_slot[slot * rows : (slot + 1) * rows]
        scaled = (piece * scale_ref[pl.ds(slab, 1), :]).astype(BF16)
        term = dot(scaled, hadamard_ref[slot], NN)
        total = total + jnp.where(slot < count, term, 0.0)
    total_ref[...] = total * (1.0 / (total_slabs * width) ** 0.5)
    chunk = 128 // slots
    for chunk_index in range(width // chunk):
        start = chunk_index * chunk
        moved_ref[chunk_index] = jnp.concatenate(
            [by_slot[s * rows : (s + 1) * rows, start : start + chunk] for s in range(slots)], axis=1
        ).astype(BF16)


def sketch_parts(tensor, counts, scale, samples):
    rows, slots, width = tensor.shape
    sketch = samples.shape[1]
    chunks = width * slots // 128
    vmem = pl.BlockSpec(memory_space=pltpu.VMEM)
    return pl.pallas_call(
        sketch_kernel,
        out_shape=(pltpu.VMEM((rows, sketch), F32), jax.ShapeDtypeStruct((chunks, rows, 128), BF16)),
        in_specs=[vmem, pl.BlockSpec(memory_space=pltpu.SMEM), vmem, vmem],
        out_specs=(vmem, vmem),
        scratch_shapes=[pltpu.VMEM((slots, width, sketch), BF16)],
        name="sketch",
    )(tensor, counts, scale, samples)


def block_inverse(tiles):
    count = len(tiles)
    size = 8 * count
    lines = list(tiles)
    sub = lax.broadcasted_iota(I32, (8, 128), 0)
    lane = lax.broadcasted_iota(I32, (8, 128), 1)

    def row_of(tile, at):
        return jnp.broadcast_to(tile[at : at + 1, :], (8, 128))

    def column_of(tile, at):
        return jnp.broadcast_to(tile[:, at : at + 1], (8, 128))

    columns = {j: [column_of(tile, j) for tile in lines] for j in range(min(AHEAD, size))}
    pivots = [jnp.ones((8, 128), F32)] * count
    for step in range(size):
        tile, at = divmod(step, 8)
        column = columns.pop(step)
        pivot = row_of(column[tile], at)
        pivots[tile] = jnp.where(sub == at, pivot, pivots[tile])
        if step == size - 1:
            break
        inverse = 1.0 / pivot
        factors = {t: column[t] * inverse for t in range(tile, count)}
        factors[tile] = jnp.where(sub > at, factors[tile], 0.0)
        if at == 7:
            factors.pop(tile)
        for later in columns.values():
            value = row_of(later[tile], at)
            for t, factor in factors.items():
                later[t] = later[t] - factor * value
        line = jnp.where(lane == step, 1.0, row_of(lines[tile], at))
        for t, factor in factors.items():
            cleared = (lane == step) if t > tile else (lane == step) & (sub > at)
            lines[t] = jnp.where(cleared, 0.0, lines[t]) - factor * line
        new = step + AHEAD
        if new < size:
            columns[new] = [
                column_of(lines[t], new) if t >= (step + 1) // 8 else None for t in range(count)
            ]
    result = []
    for t in range(count):
        inside = jnp.where(lane == sub + 8 * t, 1.0, 0.0)
        result.append(lax.rsqrt(pivots[t]) * jnp.where(lane < sub + 8 * t, lines[t], inside))
    return jnp.concatenate(result, 0)


def invert_factor(work_ref):
    size = work_ref.shape[0]
    lanes = lax.broadcasted_iota(I32, (1, size), 1)

    def spread(block):
        return jnp.concatenate([block, jnp.zeros((BLOCK, 128 - BLOCK), F32)], 1)

    diagonal = spread(work_ref[0:BLOCK, 0:BLOCK])
    for start in range(0, size, BLOCK):
        end = start + BLOCK
        after = end + BLOCK
        inverse = block_inverse([diagonal[8 * t : 8 * t + 8] for t in range(BLOCK // 8)])[:, :BLOCK]
        if end < size:
            below = dot(work_ref[end:after, start:end], inverse, NT, HIGHEST)
            diagonal = spread(work_ref[end:after, end:after] - dot(below, below, NT, HIGHEST))
            rest = dot(work_ref[end:, start:end], inverse, NT, HIGHEST)
        work_ref[start:end, :] = dot(inverse, work_ref[start:end, :], NN, HIGHEST)
        work_ref[start:end, start:end] = inverse
        if end < size:
            here = (lanes >= start) & (lanes < end)
            work_ref[end:, :] = jnp.where(here, 0.0, work_ref[end:, :]) - dot(
                rest, work_ref[start:end, :], NN, HIGHEST
            )
    row = lax.broadcasted_iota(I32, (size, size), 0)
    column = lax.broadcasted_iota(I32, (size, size), 1)
    work_ref[...] = jnp.where(row >= column, work_ref[...], 0.0)


def halves(array):
    high = array.astype(BF16)
    return high, (array - high.astype(F32)).astype(BF16)


def gram_of(pieces):
    square = cross = None
    for piece in pieces:
        flat = piece[...].reshape(-1, piece.shape[-1])
        high, rest = halves(flat)
        low = (flat - high.astype(F32) - rest.astype(F32)).astype(BF16)
        even = dot(high, high, TN) + dot(rest, rest, TN)
        odd = dot(high, rest, TN) + dot(high, low, TN)
        square = even if square is None else square + even
        cross = odd if cross is None else cross + odd
    return square + (cross + cross.T)


def gram_kernel(*refs):
    refs[-1][...] = gram_of(refs[:-1])


def factor_kernel(*refs):
    pieces, gram_ref, inverse_ref = refs[:-2], refs[-2], refs[-1]
    inverse_ref[...] = gram_ref[...] + gram_of(pieces)
    invert_factor(inverse_ref)


def core_kernel(*refs):
    pieces, (inverse_ref, moved_ref, counts_ref, basis_ref, core_ref), scratch = refs[:8], refs[8:13], refs[13:]
    rows_ref, block_ref = scratch
    blocks, parts, line, size = rows_ref.shape
    index = lax.axis_index("yz")
    core, chip = index % 2, index // 2
    chips = parts // 2
    inverse = inverse_ref[...]
    inverse_high, inverse_low = halves(inverse)
    for number, piece in enumerate(pieces):
        which, step = divmod(number, chips)
        place = 2 * ((chip + chips - STEPS[step]) % chips) + (core if which == 0 else 1 - core)
        block_ref[place] = piece[lax.axis_index("gx")]
        high, low = halves(piece[...].reshape(blocks * line, size))
        rows = dot(high, inverse_high, NT) + dot(high, inverse_low, NT) + dot(low, inverse_high, NT)
        rows_ref[:, place] = rows.reshape(blocks, line, size)
    basis_ref[...] = dot(block_ref[...].reshape(parts * line, size), inverse, NT, HIGHEST)
    every = rows_ref[...].reshape(blocks * parts * line, size).astype(BF16)
    result = dot(moved_ref[...].reshape(blocks * parts * line, 128), every, TN)
    slot = lax.broadcasted_iota(I32, result.shape, 0) // (128 // SLOTS)
    core_ref[...] = jnp.where(slot < counts_ref[index], result, 0.0).astype(BF16)


def near(*arrays):
    return tuple(pltpu.with_memory_space_constraint(each, pltpu.VMEM) for each in arrays)


def gram_part(*pieces):
    size = pieces[0].shape[-1]
    vmem = pl.BlockSpec(memory_space=pltpu.VMEM)
    return pl.pallas_call(
        gram_kernel,
        out_shape=pltpu.VMEM((size, size), F32),
        in_specs=[vmem] * len(pieces),
        out_specs=vmem,
        name="gram",
        compiler_params=ROOM,
    )(*near(*pieces))


def inverse_factor(pieces, gram):
    size = gram.shape[0]
    vmem = pl.BlockSpec(memory_space=pltpu.VMEM)
    return pl.pallas_call(
        factor_kernel,
        out_shape=pltpu.VMEM((size, size), F32),
        in_specs=[vmem] * (len(pieces) + 1),
        out_specs=vmem,
        name="factor",
        compiler_params=ROOM,
    )(*near(*pieces, gram))


def core_and_basis(pieces, inverse, moved, counts):
    blocks, line, size = pieces[0].shape
    parts = len(pieces)
    vmem = pl.BlockSpec(memory_space=pltpu.VMEM)
    return pl.pallas_call(
        core_kernel,
        out_shape=(
            jax.ShapeDtypeStruct((parts * line, size), F32),
            jax.ShapeDtypeStruct((128, size), BF16),
        ),
        in_specs=[vmem] * (parts + 2) + [pl.BlockSpec(memory_space=pltpu.SMEM)],
        out_specs=(vmem, vmem),
        scratch_shapes=[
            pltpu.VMEM((blocks, parts, line, size), F32),
            pltpu.VMEM((parts, line, size), F32),
        ],
        name="core",
        compiler_params=ROOM,
    )(*near(*pieces, inverse, moved), counts)


def local(tensor_slabs, slab_counts, column_scale, samples):
    _, slots, _ = tensor_slabs.shape
    sketch = samples.shape[1]
    blocks = lax.axis_size("gx")
    members = lax.axis_size("yz")
    swap = [(j, j ^ 1) for j in range(members)]
    total, chunks = sketch_parts(tensor_slabs, slab_counts, column_scale, samples)
    parts = lax.all_to_all(total.reshape(members, -1, sketch), "yz", 0, 0, tiled=True)
    part = jnp.broadcast_to(parts.sum(0), (blocks, *parts.shape[1:]))
    column = lax.all_to_all(part, "gx", 0, 0, tiled=True)
    pieces = [column]
    for step in STEPS[1:]:
        turn = [(j, (j + 2 * step) % members) for j in range(members)]
        pieces.append(lax.ppermute(column, "yz", turn))
    moved = lax.all_to_all(chunks, "gx", 0, 0, tiled=True)
    live = jnp.minimum(slab_counts, slots)
    pieces = pieces + [lax.ppermute(piece, "yz", swap) for piece in pieces]
    gram = gram_part(pieces[0], pieces[len(STEPS)])
    rest = [piece for number, piece in enumerate(pieces) if number % len(STEPS)]
    inverse = inverse_factor(rest, gram)
    basis, core = core_and_basis(pieces, inverse, moved, live)
    core = jnp.moveaxis(core.reshape(slots, -1, sketch), 2, 0)
    return basis, core


def solution(mesh):
    placed = (P("gx", "yz", None), P(), P(), P())
    return jax.shard_map(
        local,
        mesh=mesh,
        in_specs=placed,
        out_specs=(P("gx", None), P(None, "yz", "gx")),
        check_vma=False,
    )
```

```python
import jax
import jax.numpy as jnp
from jax import lax
from jax.experimental import pallas as pl
from jax.experimental.pallas import tpu as pltpu
from jax.sharding import PartitionSpec as P


F32, BF16, I32 = jnp.float32, jnp.bfloat16, jnp.int32
NN, NT, TN = ((1,), (0,)), ((1,), (1,)), ((0,), (0,))
HIGHEST = lax.Precision.HIGHEST
AHEAD = 9
BLOCK = 64
STEPS = (0, 2, 1, 3)
SLOTS = 4
ROOM = pltpu.CompilerParams(vmem_limit_bytes=24 << 20)


def dot(a, b, dims, precision=None):
    return lax.dot_general(
        a, b, (dims, ((), ())), precision=precision, preferred_element_type=F32
    )


def signs(rows, picked):
    both = lax.broadcasted_iota(I32, (rows, picked.shape[1]), 0) & picked
    both = both ^ (both >> 4)
    both = both ^ (both >> 2)
    both = both ^ (both >> 1)
    return (1 - 2 * (both & 1)).astype(F32)


def own_slabs(counts_ref, index, groups):
    offset = jnp.int32(0)
    for group in range(groups):
        offset = offset + jnp.where(group < index, counts_ref[group], 0)
    return offset, counts_ref[index]


def sketch_kernel(tensor_any, counts_ref, scale_any, samples_any, total_ref, moved_ref,
                  tensor_ref, scale_ref, samples_ref, hadamard_ref, sems):
    copies = [
        pltpu.make_async_copy(source, target, sems.at[number])
        for number, (source, target) in enumerate(
            ((samples_any, samples_ref), (tensor_any, tensor_ref), (scale_any, scale_ref))
        )
    ]
    for copy in copies:
        copy.start()
    rows, slots, width = tensor_ref.shape
    total_slabs, sketch = samples_ref.shape
    index = lax.axis_index("yz")
    offset, count = own_slabs(counts_ref, index, counts_ref.shape[0])
    slabs = [jnp.minimum(offset + slot, total_slabs - 1) for slot in range(slots)]
    copies[0].wait()
    for slot, slab in enumerate(slabs):
        picked = samples_ref[pl.ds(slab, 1), :]
        low = signs(32, picked & 31)
        high = signs(width // 32, picked >> 5)
        for part in range(width // 32):
            hadamard_ref[slot, pl.ds(part * 32, 32), :] = (low * high[part : part + 1, :]).astype(BF16)
    copies[1].wait()
    lines = tensor_ref[...].astype(F32).reshape(rows * slots, width).astype(BF16)
    at = lax.broadcasted_iota(I32, (rows * slots, rows * slots), 0)
    of = lax.broadcasted_iota(I32, (rows * slots, rows * slots), 1)
    pick = ((at % rows) * slots + at // rows == of).astype(F32).astype(BF16)
    by_slot = dot(pick, lines, NN)
    copies[2].wait()
    total = jnp.zeros((rows, sketch), F32)
    for slot, slab in enumerate(slabs):
        piece = by_slot[slot * rows : (slot + 1) * rows]
        scaled = (piece * scale_ref[pl.ds(slab, 1), :]).astype(BF16)
        term = dot(scaled, hadamard_ref[slot], NN)
        total = total + jnp.where(slot < count, term, 0.0)
    total_ref[...] = total * (1.0 / (total_slabs * width) ** 0.5)
    chunk = 128 // slots
    for chunk_index in range(width // chunk):
        start = chunk_index * chunk
        moved_ref[chunk_index] = jnp.concatenate(
            [by_slot[s * rows : (s + 1) * rows, start : start + chunk] for s in range(slots)], axis=1
        ).astype(BF16)


def sketch_parts(tensor, counts, scale, samples):
    rows, slots, width = tensor.shape
    sketch = samples.shape[1]
    chunks = width * slots // 128
    vmem = pl.BlockSpec(memory_space=pltpu.VMEM)
    free = pl.BlockSpec(memory_space=pl.ANY)
    return pl.pallas_call(
        sketch_kernel,
        out_shape=(pltpu.VMEM((rows, sketch), F32), jax.ShapeDtypeStruct((chunks, rows, 128), BF16)),
        in_specs=[free, pl.BlockSpec(memory_space=pltpu.SMEM), free, free],
        out_specs=(vmem, vmem),
        scratch_shapes=[
            pltpu.VMEM(tensor.shape, tensor.dtype),
            pltpu.VMEM(scale.shape, scale.dtype),
            pltpu.VMEM(samples.shape, samples.dtype),
            pltpu.VMEM((slots, width, sketch), BF16),
            pltpu.SemaphoreType.DMA((3,)),
        ],
        name="sketch",
    )(tensor, counts, scale, samples)


def block_inverse(tiles, first):
    count = len(tiles)
    size = 8 * count
    lines = list(tiles)
    sub = lax.broadcasted_iota(I32, (8, 128), 0)
    lane = lax.broadcasted_iota(I32, (8, 128), 1) - first

    def row_of(tile, at):
        return jnp.broadcast_to(tile[at : at + 1, :], (8, 128))

    def column_of(tile, at):
        return jnp.broadcast_to(tile[:, first + at : first + at + 1], (8, 128))

    columns = {j: [column_of(tile, j) for tile in lines] for j in range(min(AHEAD, size))}
    pivots = [jnp.ones((8, 128), F32)] * count
    for step in range(size):
        tile, at = divmod(step, 8)
        column = columns.pop(step)
        pivot = row_of(column[tile], at)
        pivots[tile] = jnp.where(sub == at, pivot, pivots[tile])
        if step == size - 1:
            break
        inverse = 1.0 / pivot
        factors = {t: column[t] * inverse for t in range(tile, count)}
        factors[tile] = jnp.where(sub > at, factors[tile], 0.0)
        if at == 7:
            factors.pop(tile)
        for later in columns.values():
            value = row_of(later[tile], at)
            for t, factor in factors.items():
                later[t] = later[t] - factor * value
        line = jnp.where(lane == step, 1.0, row_of(lines[tile], at))
        for t, factor in factors.items():
            cleared = (lane == step) if t > tile else (lane == step) & (sub > at)
            lines[t] = jnp.where(cleared, 0.0, lines[t]) - factor * line
        new = step + AHEAD
        if new < size:
            columns[new] = [column_of(lines[t], new) if t >= (step + 1) // 8 else None for t in range(count)]
    result = []
    for t in range(count):
        inside = jnp.where(lane == sub + 8 * t, 1.0, 0.0)
        inside = jnp.where((lane >= 0) & (lane < sub + 8 * t), lines[t], inside)
        result.append(lax.rsqrt(pivots[t]) * inside)
    return jnp.concatenate(result, 0)


def invert_factor(work_ref):
    size = work_ref.shape[0]
    lanes = lax.broadcasted_iota(I32, (1, size), 1)
    block = work_ref[0:BLOCK, 0:128]
    for start in range(0, size, BLOCK):
        end = start + BLOCK
        after = end + BLOCK
        group = start // 128 * 128
        first = start - group
        inverse = block_inverse([block[8 * t : 8 * t + 8] for t in range(BLOCK // 8)], first)
        here = (lanes >= start) & (lanes < end)
        placed = [jnp.zeros((BLOCK, 128), F32)] * (size // 128)
        placed[group // 128] = inverse
        line = jnp.where(here, jnp.concatenate(placed, 1), dot(inverse, work_ref[group : group + 128, :], NN, HIGHEST))
        if end < size:
            below = dot(work_ref[end:after, group : group + 128], inverse, NT, HIGHEST)
            new = jnp.where(here, 0.0, work_ref[end:after, :]) - dot(below, line, NN, HIGHEST)
            block = new[:, end // 128 * 128 : end // 128 * 128 + 128]
        if after < size:
            rest = dot(work_ref[after:, group : group + 128], inverse, NT, HIGHEST)
            work_ref[after:, :] = jnp.where(here, 0.0, work_ref[after:, :]) - dot(rest, line, NN, HIGHEST)
        work_ref[start:end, :] = line
        if end < size:
            work_ref[end:after, :] = new
    row = lax.broadcasted_iota(I32, (size, size), 0)
    column = lax.broadcasted_iota(I32, (size, size), 1)
    work_ref[...] = jnp.where(row >= column, work_ref[...], 0.0)


def halves(array):
    high = array.astype(BF16)
    return high, (array - high.astype(F32)).astype(BF16)


def gram_of(pieces):
    square = cross = None
    for piece in pieces:
        flat = piece[...].reshape(-1, piece.shape[-1])
        high, rest = halves(flat)
        low = (flat - high.astype(F32) - rest.astype(F32)).astype(BF16)
        even = dot(high, high, TN) + dot(rest, rest, TN)
        odd = dot(high, rest, TN) + dot(high, low, TN)
        square = even if square is None else square + even
        cross = odd if cross is None else cross + odd
    return square + (cross + cross.T)


def gram_kernel(*refs):
    refs[-1][...] = gram_of(refs[:-1])


def factor_kernel(*refs):
    pieces, gram_ref, inverse_ref = refs[:-2], refs[-2], refs[-1]
    inverse_ref[...] = gram_ref[...] + gram_of(pieces)
    invert_factor(inverse_ref)


def core_kernel(*refs):
    pieces, (inverse_ref, moved_ref, counts_ref, basis_ref, core_ref), scratch = refs[:8], refs[8:13], refs[13:]
    rows_ref, block_ref = scratch
    blocks, parts, line, size = rows_ref.shape
    index = lax.axis_index("yz")
    core, chip = index % 2, index // 2
    chips = parts // 2
    inverse = inverse_ref[...]
    inverse_high, inverse_low = halves(inverse)
    for number, piece in enumerate(pieces):
        which, step = divmod(number, chips)
        place = 2 * ((chip + chips - STEPS[step]) % chips) + (core if which == 0 else 1 - core)
        block_ref[place] = piece[lax.axis_index("gx")]
        high, low = halves(piece[...].reshape(blocks * line, size))
        rows = dot(high, inverse_high, NT) + dot(high, inverse_low, NT) + dot(low, inverse_high, NT)
        rows_ref[:, place] = rows.reshape(blocks, line, size)
    basis_ref[...] = dot(block_ref[...].reshape(parts * line, size), inverse, NT, HIGHEST)
    every = rows_ref[...].reshape(blocks * parts * line, size).astype(BF16)
    result = dot(moved_ref[...].reshape(blocks * parts * line, 128), every, TN)
    slot = lax.broadcasted_iota(I32, result.shape, 0) // (128 // SLOTS)
    core_ref[...] = jnp.where(slot < counts_ref[index], result, 0.0).astype(BF16)


def near(*arrays):
    return tuple(pltpu.with_memory_space_constraint(each, pltpu.VMEM) for each in arrays)


def gram_part(*pieces):
    size = pieces[0].shape[-1]
    vmem = pl.BlockSpec(memory_space=pltpu.VMEM)
    return pl.pallas_call(
        gram_kernel,
        out_shape=pltpu.VMEM((size, size), F32),
        in_specs=[vmem] * len(pieces),
        out_specs=vmem,
        name="gram",
        compiler_params=ROOM,
    )(*near(*pieces))


def inverse_factor(pieces, gram):
    size = gram.shape[0]
    vmem = pl.BlockSpec(memory_space=pltpu.VMEM)
    return pl.pallas_call(
        factor_kernel,
        out_shape=pltpu.VMEM((size, size), F32),
        in_specs=[vmem] * (len(pieces) + 1),
        out_specs=vmem,
        name="factor",
        compiler_params=ROOM,
    )(*near(*pieces, gram))


def core_and_basis(pieces, inverse, moved, counts):
    blocks, line, size = pieces[0].shape
    parts = len(pieces)
    vmem = pl.BlockSpec(memory_space=pltpu.VMEM)
    return pl.pallas_call(
        core_kernel,
        out_shape=(
            jax.ShapeDtypeStruct((parts * line, size), F32),
            jax.ShapeDtypeStruct((128, size), BF16),
        ),
        in_specs=[vmem] * (parts + 2) + [pl.BlockSpec(memory_space=pltpu.SMEM)],
        out_specs=(vmem, vmem),
        scratch_shapes=[
            pltpu.VMEM((blocks, parts, line, size), F32),
            pltpu.VMEM((parts, line, size), F32),
        ],
        name="core",
        compiler_params=ROOM,
    )(*near(*pieces, inverse, moved), counts)


def local(tensor_slabs, slab_counts, column_scale, samples):
    _, slots, _ = tensor_slabs.shape
    sketch = samples.shape[1]
    blocks = lax.axis_size("gx")
    members = lax.axis_size("yz")
    swap = [(j, j ^ 1) for j in range(members)]
    total, chunks = sketch_parts(tensor_slabs, slab_counts, column_scale, samples)
    parts = lax.all_to_all(total.reshape(members, -1, sketch), "yz", 0, 0, tiled=True)
    part = jnp.broadcast_to(parts.sum(0), (blocks, *parts.shape[1:]))
    column = lax.all_to_all(part, "gx", 0, 0, tiled=True)
    pieces = [column]
    for step in STEPS[1:]:
        turn = [(j, (j + 2 * step) % members) for j in range(members)]
        pieces.append(lax.ppermute(column, "yz", turn))
    moved = lax.all_to_all(chunks, "gx", 0, 0, tiled=True)
    live = jnp.minimum(slab_counts, slots)
    pieces = pieces + [lax.ppermute(piece, "yz", swap) for piece in pieces]
    gram = gram_part(pieces[0], pieces[len(STEPS)])
    rest = [piece for number, piece in enumerate(pieces) if number % len(STEPS)]
    inverse = inverse_factor(rest, gram)
    basis, core = core_and_basis(pieces, inverse, moved, live)
    core = jnp.moveaxis(core.reshape(slots, -1, sketch), 2, 0)
    return basis, core


def solution(mesh):
    placed = (P("gx", "yz", None), P(), P(), P())
    return jax.shard_map(
        local,
        mesh=mesh,
        in_specs=placed,
        out_specs=(P("gx", None), P(None, "yz", "gx")),
        check_vma=False,
    )
```

```python
import jax
import jax.numpy as jnp
from jax import lax
from jax.experimental import pallas as pl
from jax.experimental.pallas import tpu as pltpu
from jax.sharding import PartitionSpec as P


F32, BF16, I32 = jnp.float32, jnp.bfloat16, jnp.int32
NN, NT, TN = ((1,), (0,)), ((1,), (1,)), ((0,), (0,))
HIGHEST = lax.Precision.HIGHEST
AHEAD = 9
BLOCK = 64
STEPS = (0, 2, 1, 3)
EARLY = (0, 3)
SLOTS = 4
SHARES = 4
ROOM = pltpu.CompilerParams(vmem_limit_bytes=24 << 20)


def dot(a, b, dims, precision=None):
    return lax.dot_general(
        a, b, (dims, ((), ())), precision=precision, preferred_element_type=F32
    )


def signs(rows, picked):
    both = lax.broadcasted_iota(I32, (rows, picked.shape[1]), 0) & picked
    both = both ^ (both >> 4)
    both = both ^ (both >> 2)
    both = both ^ (both >> 1)
    return (1 - 2 * (both & 1)).astype(F32)


def own_slabs(counts_ref, index, groups):
    offset = jnp.int32(0)
    for group in range(groups):
        offset = offset + jnp.where(group < index, counts_ref[group], 0)
    return offset, counts_ref[index]


def lines_by_slot(tensor_ref):
    rows, slots, width = tensor_ref.shape
    lines = tensor_ref[...].astype(F32).reshape(rows * slots, width).astype(BF16)
    at = lax.broadcasted_iota(I32, (rows * slots, rows * slots), 0)
    of = lax.broadcasted_iota(I32, (rows * slots, rows * slots), 1)
    pick = ((at % rows) * slots + at // rows == of).astype(F32).astype(BF16)
    return dot(pick, lines, NN)


def sketch_kernel(tensor_ref, counts_ref, scale_ref, samples_ref, total_ref, hadamard_ref):
    rows, slots, width = tensor_ref.shape
    total_slabs, sketch = samples_ref.shape
    index = lax.axis_index("yz")
    offset, count = own_slabs(counts_ref, index, counts_ref.shape[0])
    by_slot = lines_by_slot(tensor_ref)
    total = jnp.zeros((rows, sketch), F32)
    for slot in range(slots):
        slab = jnp.minimum(offset + slot, total_slabs - 1)
        picked = samples_ref[pl.ds(slab, 1), :]
        low = signs(32, picked & 31)
        high = signs(width // 32, picked >> 5)
        for part in range(width // 32):
            hadamard_ref[slot, pl.ds(part * 32, 32), :] = (low * high[part : part + 1, :]).astype(BF16)
        piece = by_slot[slot * rows : (slot + 1) * rows]
        scaled = (piece * scale_ref[pl.ds(slab, 1), :]).astype(BF16)
        term = dot(scaled, hadamard_ref[slot], NN)
        total = total + jnp.where(slot < count, term, 0.0)
    total_ref[...] = total * (1.0 / (total_slabs * width) ** 0.5)


def spread_kernel(tensor_ref, moved_ref):
    rows, slots, width = tensor_ref.shape
    by_slot = lines_by_slot(tensor_ref)
    chunk = 128 // slots
    for chunk_index in range(width // chunk):
        start = chunk_index * chunk
        moved_ref[chunk_index] = jnp.concatenate(
            [by_slot[s * rows : (s + 1) * rows, start : start + chunk] for s in range(slots)], axis=1
        ).astype(BF16)


def sketch_part(tensor, counts, scale, samples):
    rows, slots, width = tensor.shape
    sketch = samples.shape[1]
    vmem = pl.BlockSpec(memory_space=pltpu.VMEM)
    return pl.pallas_call(
        sketch_kernel,
        out_shape=pltpu.VMEM((rows, sketch), F32),
        in_specs=[vmem, pl.BlockSpec(memory_space=pltpu.SMEM), vmem, vmem],
        out_specs=vmem,
        scratch_shapes=[pltpu.VMEM((slots, width, sketch), BF16)],
        name="sketch",
    )(tensor, counts, scale, samples)


def spread_columns(tensor):
    rows, slots, width = tensor.shape
    share = width // SHARES
    chunks = share * slots // 128
    return pl.pallas_call(
        spread_kernel,
        out_shape=jax.ShapeDtypeStruct((chunks * SHARES, rows, 128), BF16),
        grid=(SHARES,),
        in_specs=[pl.BlockSpec((rows, slots, share), lambda number: (0, 0, number))],
        out_specs=pl.BlockSpec((chunks, rows, 128), lambda number: (number, 0, 0)),
        name="spread",
    )(tensor)


def block_inverse(tiles, first):
    count = len(tiles)
    size = 8 * count
    lines = list(tiles)
    sub = lax.broadcasted_iota(I32, (8, 128), 0)
    lane = lax.broadcasted_iota(I32, (8, 128), 1) - first

    def row_of(tile, at):
        return jnp.broadcast_to(tile[at : at + 1, :], (8, 128))

    def column_of(tile, at):
        return jnp.broadcast_to(tile[:, first + at : first + at + 1], (8, 128))

    columns = {j: [column_of(tile, j) for tile in lines] for j in range(min(AHEAD, size))}
    pivots = [jnp.ones((8, 128), F32)] * count
    for step in range(size):
        tile, at = divmod(step, 8)
        column = columns.pop(step)
        pivot = row_of(column[tile], at)
        pivots[tile] = jnp.where(sub == at, pivot, pivots[tile])
        if step == size - 1:
            break
        inverse = 1.0 / pivot
        factors = {t: column[t] * inverse for t in range(tile, count)}
        factors[tile] = jnp.where(sub > at, factors[tile], 0.0)
        if at == 7:
            factors.pop(tile)
        for later in columns.values():
            value = row_of(later[tile], at)
            for t, factor in factors.items():
                later[t] = later[t] - factor * value
        line = jnp.where(lane == step, 1.0, row_of(lines[tile], at))
        for t, factor in factors.items():
            cleared = (lane == step) if t > tile else (lane == step) & (sub > at)
            lines[t] = jnp.where(cleared, 0.0, lines[t]) - factor * line
        new = step + AHEAD
        if new < size:
            columns[new] = [column_of(lines[t], new) if t >= (step + 1) // 8 else None for t in range(count)]
    result = []
    for t in range(count):
        inside = jnp.where(lane == sub + 8 * t, 1.0, 0.0)
        inside = jnp.where((lane >= 0) & (lane < sub + 8 * t), lines[t], inside)
        result.append(lax.rsqrt(pivots[t]) * inside)
    return jnp.concatenate(result, 0)


def invert_factor(work_ref):
    size = work_ref.shape[0]
    lanes = lax.broadcasted_iota(I32, (1, size), 1)
    block = work_ref[0:BLOCK, 0:128]
    for start in range(0, size, BLOCK):
        end = start + BLOCK
        after = end + BLOCK
        group = start // 128 * 128
        first = start - group
        inverse = block_inverse([block[8 * t : 8 * t + 8] for t in range(BLOCK // 8)], first)
        here = (lanes >= start) & (lanes < end)
        placed = [jnp.zeros((BLOCK, 128), F32)] * (size // 128)
        placed[group // 128] = inverse
        line = jnp.where(here, jnp.concatenate(placed, 1), dot(inverse, work_ref[group : group + 128, :], NN, HIGHEST))
        if end < size:
            below = dot(work_ref[end:after, group : group + 128], inverse, NT, HIGHEST)
            new = jnp.where(here, 0.0, work_ref[end:after, :]) - dot(below, line, NN, HIGHEST)
            block = new[:, end // 128 * 128 : end // 128 * 128 + 128]
        if after < size:
            rest = dot(work_ref[after:, group : group + 128], inverse, NT, HIGHEST)
            work_ref[after:, :] = jnp.where(here, 0.0, work_ref[after:, :]) - dot(rest, line, NN, HIGHEST)
        work_ref[start:end, :] = line
        if end < size:
            work_ref[end:after, :] = new
    row = lax.broadcasted_iota(I32, (size, size), 0)
    column = lax.broadcasted_iota(I32, (size, size), 1)
    work_ref[...] = jnp.where(row >= column, work_ref[...], 0.0)


def halves(array):
    high = array.astype(BF16)
    return high, (array - high.astype(F32)).astype(BF16)


def gram_of(pieces):
    square = cross = None
    for piece in pieces:
        flat = piece[...].reshape(-1, piece.shape[-1])
        high, rest = halves(flat)
        low = (flat - high.astype(F32) - rest.astype(F32)).astype(BF16)
        even = dot(high, high, TN) + dot(rest, rest, TN)
        odd = dot(high, rest, TN) + dot(high, low, TN)
        square = even if square is None else square + even
        cross = odd if cross is None else cross + odd
    return square + (cross + cross.T)


def gram_kernel(*refs):
    refs[-1][...] = gram_of(refs[:-1])


def factor_kernel(*refs):
    pieces, gram_ref, inverse_ref = refs[:-2], refs[-2], refs[-1]
    inverse_ref[...] = gram_ref[...] + gram_of(pieces)
    invert_factor(inverse_ref)


def core_kernel(*refs):
    pieces, (inverse_ref, moved_ref, counts_ref, basis_ref, core_ref), scratch = refs[:8], refs[8:13], refs[13:]
    rows_ref, block_ref = scratch
    blocks, parts, line, size = rows_ref.shape
    index = lax.axis_index("yz")
    core, chip = index % 2, index // 2
    chips = parts // 2
    inverse = inverse_ref[...]
    inverse_high, inverse_low = halves(inverse)
    for number, piece in enumerate(pieces):
        which, step = divmod(number, chips)
        place = 2 * ((chip + chips - STEPS[step]) % chips) + (core if which == 0 else 1 - core)
        block_ref[place] = piece[lax.axis_index("gx")]
        high, low = halves(piece[...].reshape(blocks * line, size))
        rows = dot(high, inverse_high, NT) + dot(high, inverse_low, NT) + dot(low, inverse_high, NT)
        rows_ref[:, place] = rows.reshape(blocks, line, size)
    basis_ref[...] = dot(block_ref[...].reshape(parts * line, size), inverse, NT, HIGHEST)
    every = rows_ref[...].reshape(blocks * parts * line, size).astype(BF16)
    result = dot(moved_ref[...].reshape(blocks * parts * line, 128), every, TN)
    slot = lax.broadcasted_iota(I32, result.shape, 0) // (128 // SLOTS)
    core_ref[...] = jnp.where(slot < counts_ref[index], result, 0.0).astype(BF16)


def near(*arrays):
    return tuple(pltpu.with_memory_space_constraint(each, pltpu.VMEM) for each in arrays)


def gram_part(*pieces):
    size = pieces[0].shape[-1]
    vmem = pl.BlockSpec(memory_space=pltpu.VMEM)
    return pl.pallas_call(
        gram_kernel,
        out_shape=pltpu.VMEM((size, size), F32),
        in_specs=[vmem] * len(pieces),
        out_specs=vmem,
        name="gram",
        compiler_params=ROOM,
    )(*near(*pieces))


def inverse_factor(pieces, gram):
    size = gram.shape[0]
    vmem = pl.BlockSpec(memory_space=pltpu.VMEM)
    return pl.pallas_call(
        factor_kernel,
        out_shape=pltpu.VMEM((size, size), F32),
        in_specs=[vmem] * (len(pieces) + 1),
        out_specs=vmem,
        name="factor",
        compiler_params=ROOM,
    )(*near(*pieces, gram))


def core_and_basis(pieces, inverse, moved, counts):
    blocks, line, size = pieces[0].shape
    parts = len(pieces)
    vmem = pl.BlockSpec(memory_space=pltpu.VMEM)
    return pl.pallas_call(
        core_kernel,
        out_shape=(
            jax.ShapeDtypeStruct((parts * line, size), F32),
            jax.ShapeDtypeStruct((128, size), BF16),
        ),
        in_specs=[vmem] * (parts + 2) + [pl.BlockSpec(memory_space=pltpu.SMEM)],
        out_specs=(vmem, vmem),
        scratch_shapes=[
            pltpu.VMEM((blocks, parts, line, size), F32),
            pltpu.VMEM((parts, line, size), F32),
        ],
        name="core",
        compiler_params=ROOM,
    )(*near(*pieces, inverse, moved), counts)


def local(tensor_slabs, slab_counts, column_scale, samples):
    _, slots, _ = tensor_slabs.shape
    sketch = samples.shape[1]
    blocks = lax.axis_size("gx")
    members = lax.axis_size("yz")
    swap = [(j, j ^ 1) for j in range(members)]
    total = sketch_part(tensor_slabs, slab_counts, column_scale, samples)
    parts = lax.all_to_all(total.reshape(members, -1, sketch), "yz", 0, 0, tiled=True)
    part = jnp.broadcast_to(parts.sum(0), (blocks, *parts.shape[1:]))
    column = lax.all_to_all(part, "gx", 0, 0, tiled=True)
    pieces = [column]
    for step in STEPS[1:]:
        turn = [(j, (j + 2 * step) % members) for j in range(members)]
        pieces.append(lax.ppermute(column, "yz", turn))
    chunks = spread_columns(tensor_slabs)
    moved = lax.all_to_all(chunks, "gx", 0, 0, tiled=True)
    live = jnp.minimum(slab_counts, slots)
    pieces = pieces + [lax.ppermute(piece, "yz", swap) for piece in pieces]
    gram = gram_part(*(piece for number, piece in enumerate(pieces) if number % len(STEPS) in EARLY))
    rest = [piece for number, piece in enumerate(pieces) if number % len(STEPS) not in EARLY]
    inverse = inverse_factor(rest, gram)
    basis, core = core_and_basis(pieces, inverse, moved, live)
    core = jnp.moveaxis(core.reshape(slots, -1, sketch), 2, 0)
    return basis, core


def solution(mesh):
    placed = (P("gx", "yz", None), P(), P(), P())
    return jax.shard_map(
        local,
        mesh=mesh,
        in_specs=placed,
        out_specs=(P("gx", None), P(None, "yz", "gx")),
        check_vma=False,
    )
```

```python
import jax
import jax.numpy as jnp
from jax import lax
from jax.experimental import pallas as pl
from jax.experimental.pallas import tpu as pltpu
from jax.sharding import PartitionSpec as P


F32, BF16, I32 = jnp.float32, jnp.bfloat16, jnp.int32
NN, NT, TN = ((1,), (0,)), ((1,), (1,)), ((0,), (0,))
HIGHEST = lax.Precision.HIGHEST
AHEAD = 9
BLOCK = 64
STEPS = (0, 2, 1, 3)
EARLY = (0, 3)
SLOTS = 4
ROOM = pltpu.CompilerParams(vmem_limit_bytes=24 << 20)


def dot(a, b, dims, precision=None):
    return lax.dot_general(
        a, b, (dims, ((), ())), precision=precision, preferred_element_type=F32
    )


def signs(rows, picked):
    both = lax.broadcasted_iota(I32, (rows, picked.shape[1]), 0) & picked
    both = both ^ (both >> 4)
    both = both ^ (both >> 2)
    both = both ^ (both >> 1)
    return (1 - 2 * (both & 1)).astype(F32)


def own_slabs(counts_ref, index, groups):
    offset = jnp.int32(0)
    for group in range(groups):
        offset = offset + jnp.where(group < index, counts_ref[group], 0)
    return offset, counts_ref[index]


def lines_by_slot(tensor_ref):
    rows, slots, width = tensor_ref.shape
    lines = tensor_ref[...].astype(F32).reshape(rows * slots, width).astype(BF16)
    at = lax.broadcasted_iota(I32, (rows * slots, rows * slots), 0)
    of = lax.broadcasted_iota(I32, (rows * slots, rows * slots), 1)
    pick = ((at % rows) * slots + at // rows == of).astype(F32).astype(BF16)
    return dot(pick, lines, NN)


def sketch_kernel(tensor_ref, counts_ref, scale_ref, samples_ref, total_ref, hadamard_ref):
    rows, slots, width = tensor_ref.shape
    total_slabs, sketch = samples_ref.shape
    index = lax.axis_index("yz")
    offset, count = own_slabs(counts_ref, index, counts_ref.shape[0])
    by_slot = lines_by_slot(tensor_ref)
    total = jnp.zeros((rows, sketch), F32)
    for slot in range(slots):
        slab = jnp.minimum(offset + slot, total_slabs - 1)
        picked = samples_ref[pl.ds(slab, 1), :]
        low = signs(32, picked & 31)
        high = signs(width // 32, picked >> 5)
        for part in range(width // 32):
            hadamard_ref[slot, pl.ds(part * 32, 32), :] = (low * high[part : part + 1, :]).astype(BF16)
        piece = by_slot[slot * rows : (slot + 1) * rows]
        scaled = (piece * scale_ref[pl.ds(slab, 1), :]).astype(BF16)
        term = dot(scaled, hadamard_ref[slot], NN)
        total = total + jnp.where(slot < count, term, 0.0)
    total_ref[...] = total * (1.0 / (total_slabs * width) ** 0.5)


def spread_kernel(tensor_ref, moved_ref):
    rows, slots, width = tensor_ref.shape
    by_slot = lines_by_slot(tensor_ref)
    chunk = 128 // slots
    for chunk_index in range(width // chunk):
        start = chunk_index * chunk
        moved_ref[chunk_index] = jnp.concatenate(
            [by_slot[s * rows : (s + 1) * rows, start : start + chunk] for s in range(slots)], axis=1
        ).astype(BF16)


def sketch_part(tensor, counts, scale, samples):
    rows, slots, width = tensor.shape
    sketch = samples.shape[1]
    vmem = pl.BlockSpec(memory_space=pltpu.VMEM)
    return pl.pallas_call(
        sketch_kernel,
        out_shape=pltpu.VMEM((rows, sketch), F32),
        in_specs=[vmem, pl.BlockSpec(memory_space=pltpu.SMEM), vmem, vmem],
        out_specs=vmem,
        scratch_shapes=[pltpu.VMEM((slots, width, sketch), BF16)],
        name="sketch",
    )(tensor, counts, scale, samples)


def spread_columns(tensor):
    rows, slots, width = tensor.shape
    vmem = pl.BlockSpec(memory_space=pltpu.VMEM)
    return pl.pallas_call(
        spread_kernel,
        out_shape=jax.ShapeDtypeStruct((width * slots // 128, rows, 128), BF16),
        in_specs=[vmem],
        out_specs=vmem,
        name="spread",
        compiler_params=ROOM,
    )(tensor)


def block_inverse(tiles, first):
    count = len(tiles)
    size = 8 * count
    lines = list(tiles)
    sub = lax.broadcasted_iota(I32, (8, 128), 0)
    lane = lax.broadcasted_iota(I32, (8, 128), 1) - first

    def row_of(tile, at):
        return jnp.broadcast_to(tile[at : at + 1, :], (8, 128))

    def column_of(tile, at):
        return jnp.broadcast_to(tile[:, first + at : first + at + 1], (8, 128))

    columns = {j: [column_of(tile, j) for tile in lines] for j in range(min(AHEAD, size))}
    pivots = [jnp.ones((8, 128), F32)] * count
    for step in range(size):
        tile, at = divmod(step, 8)
        column = columns.pop(step)
        pivot = row_of(column[tile], at)
        pivots[tile] = jnp.where(sub == at, pivot, pivots[tile])
        if step == size - 1:
            break
        inverse = 1.0 / pivot
        factors = {t: column[t] * inverse for t in range(tile, count)}
        factors[tile] = jnp.where(sub > at, factors[tile], 0.0)
        if at == 7:
            factors.pop(tile)
        for later in columns.values():
            value = row_of(later[tile], at)
            for t, factor in factors.items():
                later[t] = later[t] - factor * value
        line = jnp.where(lane == step, 1.0, row_of(lines[tile], at))
        for t, factor in factors.items():
            cleared = (lane == step) if t > tile else (lane == step) & (sub > at)
            lines[t] = jnp.where(cleared, 0.0, lines[t]) - factor * line
        new = step + AHEAD
        if new < size:
            columns[new] = [column_of(lines[t], new) if t >= (step + 1) // 8 else None for t in range(count)]
    result = []
    for t in range(count):
        inside = jnp.where(lane == sub + 8 * t, 1.0, 0.0)
        inside = jnp.where((lane >= 0) & (lane < sub + 8 * t), lines[t], inside)
        result.append(lax.rsqrt(pivots[t]) * inside)
    return jnp.concatenate(result, 0)


def invert_factor(work_ref):
    size = work_ref.shape[0]
    lanes = lax.broadcasted_iota(I32, (1, size), 1)
    block = work_ref[0:BLOCK, 0:128]
    for start in range(0, size, BLOCK):
        end = start + BLOCK
        after = end + BLOCK
        group = start // 128 * 128
        first = start - group
        inverse = block_inverse([block[8 * t : 8 * t + 8] for t in range(BLOCK // 8)], first)
        here = (lanes >= start) & (lanes < end)
        placed = [jnp.zeros((BLOCK, 128), F32)] * (size // 128)
        placed[group // 128] = inverse
        line = jnp.where(here, jnp.concatenate(placed, 1), dot(inverse, work_ref[group : group + 128, :], NN, HIGHEST))
        if end < size:
            below = dot(work_ref[end:after, group : group + 128], inverse, NT, HIGHEST)
            new = jnp.where(here, 0.0, work_ref[end:after, :]) - dot(below, line, NN, HIGHEST)
            block = new[:, end // 128 * 128 : end // 128 * 128 + 128]
        if after < size:
            rest = dot(work_ref[after:, group : group + 128], inverse, NT, HIGHEST)
            work_ref[after:, :] = jnp.where(here, 0.0, work_ref[after:, :]) - dot(rest, line, NN, HIGHEST)
        work_ref[start:end, :] = line
        if end < size:
            work_ref[end:after, :] = new
    row = lax.broadcasted_iota(I32, (size, size), 0)
    column = lax.broadcasted_iota(I32, (size, size), 1)
    work_ref[...] = jnp.where(row >= column, work_ref[...], 0.0)


def halves(array):
    high = array.astype(BF16)
    return high, (array - high.astype(F32)).astype(BF16)


def gram_of(pieces):
    square = cross = None
    for piece in pieces:
        flat = piece[...].reshape(-1, piece.shape[-1])
        high, rest = halves(flat)
        low = (flat - high.astype(F32) - rest.astype(F32)).astype(BF16)
        even = dot(high, high, TN) + dot(rest, rest, TN)
        odd = dot(high, rest, TN) + dot(high, low, TN)
        square = even if square is None else square + even
        cross = odd if cross is None else cross + odd
    return square + (cross + cross.T)


def gram_kernel(*refs):
    refs[-1][...] = gram_of(refs[:-1])


def factor_kernel(*refs):
    pieces, gram_ref, inverse_ref = refs[:-2], refs[-2], refs[-1]
    inverse_ref[...] = gram_ref[...] + gram_of(pieces)
    invert_factor(inverse_ref)


def core_kernel(*refs):
    pieces, (inverse_ref, moved_ref, counts_ref, basis_ref, core_ref), scratch = refs[:8], refs[8:13], refs[13:]
    rows_ref, block_ref = scratch
    blocks, parts, line, size = rows_ref.shape
    index = lax.axis_index("yz")
    core, chip = index % 2, index // 2
    chips = parts // 2
    inverse = inverse_ref[...]
    inverse_high, inverse_low = halves(inverse)
    for number, piece in enumerate(pieces):
        which, step = divmod(number, chips)
        place = 2 * ((chip + chips - STEPS[step]) % chips) + (core if which == 0 else 1 - core)
        block_ref[place] = piece[lax.axis_index("gx")]
        high, low = halves(piece[...].reshape(blocks * line, size))
        rows = dot(high, inverse_high, NT) + dot(high, inverse_low, NT) + dot(low, inverse_high, NT)
        rows_ref[:, place] = rows.reshape(blocks, line, size)
    basis_ref[...] = dot(block_ref[...].reshape(parts * line, size), inverse, NT, HIGHEST)
    every = rows_ref[...].reshape(blocks * parts * line, size).astype(BF16)
    result = dot(moved_ref[...].reshape(blocks * parts * line, 128), every, TN)
    slot = lax.broadcasted_iota(I32, result.shape, 0) // (128 // SLOTS)
    core_ref[...] = jnp.where(slot < counts_ref[index], result, 0.0).astype(BF16)


def near(*arrays):
    return tuple(pltpu.with_memory_space_constraint(each, pltpu.VMEM) for each in arrays)


def gram_part(*pieces):
    size = pieces[0].shape[-1]
    vmem = pl.BlockSpec(memory_space=pltpu.VMEM)
    return pl.pallas_call(
        gram_kernel,
        out_shape=pltpu.VMEM((size, size), F32),
        in_specs=[vmem] * len(pieces),
        out_specs=vmem,
        name="gram",
        compiler_params=ROOM,
    )(*near(*pieces))


def inverse_factor(pieces, gram):
    size = gram.shape[0]
    vmem = pl.BlockSpec(memory_space=pltpu.VMEM)
    return pl.pallas_call(
        factor_kernel,
        out_shape=pltpu.VMEM((size, size), F32),
        in_specs=[vmem] * (len(pieces) + 1),
        out_specs=vmem,
        name="factor",
        compiler_params=ROOM,
    )(*near(*pieces, gram))


def core_and_basis(pieces, inverse, moved, counts):
    blocks, line, size = pieces[0].shape
    parts = len(pieces)
    vmem = pl.BlockSpec(memory_space=pltpu.VMEM)
    return pl.pallas_call(
        core_kernel,
        out_shape=(
            jax.ShapeDtypeStruct((parts * line, size), F32),
            jax.ShapeDtypeStruct((128, size), BF16),
        ),
        in_specs=[vmem] * (parts + 2) + [pl.BlockSpec(memory_space=pltpu.SMEM)],
        out_specs=(vmem, vmem),
        scratch_shapes=[
            pltpu.VMEM((blocks, parts, line, size), F32),
            pltpu.VMEM((parts, line, size), F32),
        ],
        name="core",
        compiler_params=ROOM,
    )(*near(*pieces, inverse, moved), counts)


def local(tensor_slabs, slab_counts, column_scale, samples):
    _, slots, _ = tensor_slabs.shape
    sketch = samples.shape[1]
    blocks = lax.axis_size("gx")
    members = lax.axis_size("yz")
    swap = [(j, j ^ 1) for j in range(members)]
    total = sketch_part(tensor_slabs, slab_counts, column_scale, samples)
    parts = lax.all_to_all(total.reshape(members, -1, sketch), "yz", 0, 0, tiled=True)
    part = jnp.broadcast_to(parts.sum(0), (blocks, *parts.shape[1:]))
    column = lax.all_to_all(part, "gx", 0, 0, tiled=True)
    pieces = [column]
    for step in STEPS[1:]:
        turn = [(j, (j + 2 * step) % members) for j in range(members)]
        pieces.append(lax.ppermute(column, "yz", turn))
    chunks = spread_columns(tensor_slabs)
    moved = lax.all_to_all(chunks, "gx", 0, 0, tiled=True)
    live = jnp.minimum(slab_counts, slots)
    pieces = pieces + [lax.ppermute(piece, "yz", swap) for piece in pieces]
    gram = gram_part(*(piece for number, piece in enumerate(pieces) if number % len(STEPS) in EARLY))
    rest = [piece for number, piece in enumerate(pieces) if number % len(STEPS) not in EARLY]
    inverse = inverse_factor(rest, gram)
    basis, core = core_and_basis(pieces, inverse, moved, live)
    core = jnp.moveaxis(core.reshape(slots, -1, sketch), 2, 0)
    return basis, core


def solution(mesh):
    placed = (P("gx", "yz", None), P(), P(), P())
    return jax.shard_map(
        local,
        mesh=mesh,
        in_specs=placed,
        out_specs=(P("gx", None), P(None, "yz", "gx")),
        check_vma=False,
    )
```
